128 devices in a mesh: dp: 16 (over z, y_hi, core), section: 2 (over y_lo), mp: 4 (over x).
Axes of the slice: x: 4, y: 4 (y_hi: 2, y_lo: 2; y = y_hi * 2 + y_lo), z: 4, core: 2. Of those that a mesh axis runs over, the one named last changes fastest.
Arguments:
- patches: bfloat16 [16, 2, 16, 16, 3200], P('dp', 'section'), may hold values from -6 to 6
- w_in: bfloat16 [3200, 3584], P(None, 'mp'), may hold values from -0.109375 to 0.109375
- ln_gain: float32 [3584], P('mp'), may hold values from 0.25 to 1.75
- ln_bias: float32 [3584], P('mp'), may hold values from -3 to 3
- dw_kernel: float32 [3, 3, 3584], P(None, None, 'mp'), may hold values from -2 to 2
- w_tube: bfloat16 [2, 2, 2, 3584, 3584], P('section', None, None, 'mp', 'dp'), may hold values from -0.03125 to 0.03125
- grad_out: bfloat16 [16, 64, 3584], P(None, None, 'dp'), may hold values from -6 to 6
- clip_frames: int32 [16], replicated, may hold values from 8 to 32, as said below
- clip_batch: int32 [16], replicated, may hold values from 0 to 3
Outputs:
- tubes: bfloat16 [16, 64, 3584], P(None, ('section', 'mp'), 'dp')
- grad_w_in: float32 [3200, 3584], P(None, ('mp', 'dp', 'section'))
- grad_gain: float32 [3584], P(('mp', 'dp', 'section'))
- grad_bias: float32 [3584], P(('mp', 'dp', 'section'))
- grad_dw: float32 [3, 3, 3584], P(None, None, ('mp', 'dp', 'section'))
- grad_w_tube: float32 [2, 2, 2, 3584, 3584], P('section', None, None, 'mp', 'dp')
The draws below stay inside these ranges and needn't reach their ends.
Inputs may be any that keep to these rules, and one draw needn't show every extreme that they name: `clip_frames`: even numbers; their halves sum to 16 or more.
All inputs are finite; a program needn't handle non-finite values.
Results may differ from the reference program's by a relative error of at most 0.005.
Values may be sent and summed in bfloat16 or wider, within the bound.
A program may use at most 128 MiB of HBM per device.

```python
import jax
import jax.numpy as jnp
from jax import lax

D_IN = 3200
CH = 3584
GRID = 16
MICRO = 4
NPAIR = 16
NCLIP = 16


def draw_clip_frames(key, part):
    first, second = jax.random.split(key)
    halves = jax.random.randint(first, (NCLIP,), 4, 17)
    order = jax.random.permutation(second, NCLIP)
    halves = halves.at[order[0]].set(16)
    if NCLIP > 1:
        halves = halves.at[order[1]].set(4)
    return (2 * halves).astype(jnp.int32)


def plant(entries, own_key, least, top_value):
    index_at = [jax.random.randint(jax.random.fold_in(own_key, axis), (), 0, length) for axis, length in enumerate(entries.shape)]
    widest = entries.shape.index(max(entries.shape))
    next_to = index_at[:widest] + [(index_at[widest] + 1) % entries.shape[widest]] + index_at[widest + 1:]
    return entries.at[tuple(index_at)].set(least).at[tuple(next_to)].set(top_value)


def block_levels(own_key, dims, pieces, least, top_value):
    loudness, own = 1.0, jax.random.fold_in(own_key, 6)
    for axis_at, shards_of in pieces:
        draws = jnp.exp(jax.random.uniform(jax.random.fold_in(own, axis_at), (shards_of,), jnp.float32, least / len(pieces), top_value / len(pieces)))
        loudness = loudness * jnp.repeat(draws, dims[axis_at] // shards_of).reshape([-1 if axis == axis_at else 1 for axis in range(len(dims))])
    return loudness


def gaussian(key, dims, spread, most, cuts=(), kind=jnp.bfloat16):
    loudness = block_levels(key, dims, cuts, -0.22, 0.18) if cuts else 1.0
    entries = jax.random.normal(key, dims, jnp.float32) * spread * loudness
    return jnp.minimum(jnp.maximum(entries, -most), most).astype(kind)


def setup_inputs(seed: int = 0) -> dict:
    seeds = jax.random.split(jax.random.key(seed), 10)
    patches = gaussian(seeds[0], (NPAIR, 2, GRID, GRID, D_IN), 1.0, 6.0, ((0, 16), (1, 2)))
    w_in = gaussian(seeds[1], (D_IN, CH), D_IN ** -0.5, 0.109375, ((1, 4),))
    ln_gain = jnp.clip(1.0 + 0.15 * jax.random.normal(seeds[2], (CH,), jnp.float32), 0.25, 1.75)
    ln_bias = gaussian(seeds[3], (CH,), 0.5, 3.0, ((0, 4),), jnp.float32)
    dw_kernel = gaussian(seeds[4], (3, 3, CH), 9 ** -0.5, 2.0, ((2, 4),), jnp.float32)
    w_tube = gaussian(seeds[5], (2, 2, 2, CH, CH), (8 * CH) ** -0.5, 0.03125, ((0, 2), (3, 4), (4, 16)))
    grad_out = gaussian(seeds[6], (NPAIR, (GRID // 2) * (GRID // 2), CH), 1.0, 6.0, ((2, 16),))
    clip_frames = draw_clip_frames(jax.random.fold_in(seeds[9], 71), 0)
    clip_batch = plant(jax.random.randint(seeds[8], (NCLIP,), 0, MICRO), jax.random.fold_in(seeds[8], 1), 0, MICRO - 1).astype(jnp.int32)
    return {"patches": patches, "w_in": w_in, "ln_gain": ln_gain, "ln_bias": ln_bias, "dw_kernel": dw_kernel, "w_tube": w_tube, "grad_out": grad_out, "clip_frames": clip_frames, "clip_batch": clip_batch}


EPS = 1e-06

def silu_slope(value):
    sig = jax.nn.sigmoid(value)
    return sig * (1.0 + value * (1.0 - sig))

def pair_scale(clip_frames, clip_batch, count, nclip):
    halves = (clip_frames // 2).astype(jnp.int32)
    ends = jnp.cumsum(halves).astype(jnp.int32)
    starts = (ends - halves).astype(jnp.int32)
    places = jnp.arange(count, dtype=jnp.int32)
    member = ((places[:, None] >= starts[None, :]) & (places[:, None] < ends[None, :])).astype(jnp.float32)
    batch_hot = (clip_batch[:, None] == jnp.arange(MICRO, dtype=jnp.int32)[None, :]).astype(jnp.float32)
    batch_pairs = lax.optimization_barrier(jnp.sum(batch_hot * halves.astype(jnp.float32)[:, None], axis=0))
    clip_load = lax.optimization_barrier(jnp.sum(batch_hot * batch_pairs[None, :], axis=1))
    clip_scale = 10.0 * nclip / (MICRO * clip_load)
    return lax.optimization_barrier(jnp.sum(member * clip_scale[None, :], axis=1))

def reference(patches, w_in, ln_gain, ln_bias, dw_kernel, w_tube, grad_out, clip_frames, clip_batch):
    half = GRID // 2
    rows = patches.reshape(NPAIR * 2 * GRID * GRID, D_IN)
    pre = jnp.dot(rows, w_in, preferred_element_type=jnp.float32)
    mean = lax.optimization_barrier(jnp.mean(pre, axis=1, keepdims=True))
    centered = pre - mean
    var = lax.optimization_barrier(jnp.mean(centered * centered, axis=1, keepdims=True))
    rstd = lax.rsqrt(var + EPS)
    normed = centered * rstd
    shifted = normed * ln_gain + ln_bias
    act = jax.nn.silu(shifted).reshape(NPAIR * 2, GRID, GRID, CH)
    padded = jnp.pad(act, ((0, 0), (1, 1), (1, 1), (0, 0)))
    mixed = jnp.zeros_like(act)
    for upos in range(3):
        for vpos in range(3):
            mixed = mixed + dw_kernel[upos, vpos] * padded[:, upos:upos + GRID, vpos:vpos + GRID]
    maps = (act + jax.nn.silu(mixed)).astype(jnp.bfloat16)
    blocks = maps.reshape(NPAIR, 2, half, 2, half, 2, CH).transpose(0, 2, 4, 1, 3, 5, 6).reshape(NPAIR * half * half, 8 * CH)
    kernel = w_tube.reshape(8 * CH, CH)
    tubes = jnp.dot(blocks, kernel, preferred_element_type=jnp.float32).astype(jnp.bfloat16).reshape(NPAIR, half * half, CH)
    weight = pair_scale(clip_frames, clip_batch, NPAIR, NCLIP)
    upstream = (grad_out.astype(jnp.float32) * weight[:, None, None]).astype(jnp.bfloat16).reshape(NPAIR * half * half, CH)
    grad_w_tube = lax.dot_general(blocks, upstream, (((0,), (0,)), ((), ())), preferred_element_type=jnp.float32).reshape(2, 2, 2, CH, CH)
    grad_blocks = lax.dot_general(upstream, kernel, (((1,), (1,)), ((), ())), preferred_element_type=jnp.float32)
    grad_maps = grad_blocks.reshape(NPAIR, half, half, 2, 2, 2, CH).transpose(0, 3, 1, 4, 2, 5, 6).reshape(NPAIR * 2, GRID, GRID, CH)
    grad_mixed = grad_maps * silu_slope(mixed)
    grad_pad = jnp.pad(grad_mixed, ((0, 0), (1, 1), (1, 1), (0, 0)))
    grad_act = grad_maps
    kernel_rows = []
    for upos in range(3):
        for vpos in range(3):
            grad_act = grad_act + dw_kernel[upos, vpos] * grad_pad[:, 2 - upos:2 - upos + GRID, 2 - vpos:2 - vpos + GRID]
            kernel_rows.append(lax.optimization_barrier(jnp.sum(grad_mixed * padded[:, upos:upos + GRID, vpos:vpos + GRID], axis=(0, 1, 2))))
    grad_dw = jnp.stack(kernel_rows).reshape(3, 3, CH)
    grad_shift = grad_act.reshape(-1, CH) * silu_slope(shifted)
    grad_gain = lax.optimization_barrier(jnp.sum(grad_shift * normed, axis=0))
    grad_bias = lax.optimization_barrier(jnp.sum(grad_shift, axis=0))
    scaled = grad_shift * ln_gain
    grad_pre = (scaled - lax.optimization_barrier(jnp.mean(scaled, axis=1, keepdims=True)) - normed * lax.optimization_barrier(jnp.mean(scaled * normed, axis=1, keepdims=True))) * rstd
    grad_w_in = lax.dot_general(rows, grad_pre.astype(jnp.bfloat16), (((0,), (0,)), ((), ())), preferred_element_type=jnp.float32)
    return (tubes, grad_w_in, grad_gain, grad_bias, grad_dw, grad_w_tube)
```

```python
import jax
import jax.numpy as jnp
from jax import lax
from jax.experimental import pallas as pl
from jax.experimental.pallas import tpu as pltpu
from jax.sharding import PartitionSpec as P

MESH = pl.DeviceIdType.MESH
F32 = jnp.float32
BF16 = jnp.bfloat16

CH = 3584
EPS = 1e-06
W = 896
D = 3200
OW = 224
TOK = 256
DX = D + 128
HX = DX // 2
LANES = 128
NB = W // LANES


class Place:
    def __init__(self):
        dp = lax.axis_index("dp")
        self.z = dp // 4
        self.yh = (dp // 2) % 2
        self.core = dp % 2
        self.sec = lax.axis_index("section")
        self.mp = lax.axis_index("mp")
        self.y = self.yh * 2 + self.sec

    def at(self, z, yh, core):
        return (z * 4 + yh * 2 + core, self.sec, self.mp)

    def zmove(self, k):
        return self.at((self.z + k) % 4, self.yh, self.core)

    def partner(self):
        return self.at(self.z, self.yh, 1 - self.core)

    def yhflip(self):
        return self.at(self.z, 1 - self.yh, self.core)

    def ymove(self, k):
        y = (self.y + k) % 4
        return (self.z * 4 + (y // 2) * 2 + self.core, y % 2, self.mp)

    def mpmove(self, k):
        return (self.z * 4 + self.yh * 2 + self.core, self.sec, (self.mp + k) % 4)


def greet(devices):
    barrier = pltpu.get_barrier_semaphore()
    for dev in devices:
        pl.semaphore_signal(barrier, inc=1, device_id=dev, device_id_type=MESH)
    pl.semaphore_wait(barrier, len(devices))


def remote(src, dst, send, recv, dev):
    return pltpu.make_async_remote_copy(
        src_ref=src, dst_ref=dst, send_sem=send, recv_sem=recv, device_id=dev, device_id_type=MESH
    )


def lanes(b):
    return pl.ds(pl.multiple_of(b * LANES, LANES), LANES)


def sigmoid(v):
    return 1.0 / (1.0 + jnp.exp(-v))


def shift_j(plane, d):
    if d == 0:
        return plane
    row = lax.broadcasted_iota(jnp.int32, plane.shape, 0) % 8
    if d < 0:
        return jnp.where(row == 0, 0.0, pltpu.roll(plane, 1, 0))
    return jnp.where(row == 7, 0.0, pltpu.roll(plane, plane.shape[0] - 1, 0))


def shift_i(plane, d):
    if d == 0:
        return plane
    blank = jnp.zeros((8, plane.shape[1]), plane.dtype)
    if d < 0:
        return jnp.concatenate([blank, plane[:-8]], axis=0)
    return jnp.concatenate([plane[8:], blank], axis=0)


def neighbours(planes):
    moved = {}

    def get(s, t):
        us, di = s % 2, s // 2
        vs, dj = t % 2, t // 2
        if (us, vs, dj) not in moved:
            moved[us, vs, dj] = shift_j(planes[us][vs], dj)
        return shift_i(moved[us, vs, dj], di)

    return get


def across(rows, width):
    return jnp.transpose(rows)[:width]


def down(row):
    return jnp.transpose(jnp.broadcast_to(row, (LANES, row.shape[1])))


def lane_sum(x):
    return jnp.sum(x, axis=1, keepdims=True)


def two_parts(x):
    full = x + pltpu.roll(x, 64, 1)
    high = full.astype(BF16).astype(F32)
    lane = lax.broadcasted_iota(jnp.int32, x.shape, 1)
    return jnp.where(lane < 64, high, full - high).astype(BF16)


def to_link(x, grad):
    if grad == x.shape[1]:
        return x.astype(BF16)
    return jnp.concatenate([x[:, :grad].astype(BF16), two_parts(x[:, grad:])], axis=1)


def pick_lane(first, second):
    lane = lax.broadcasted_iota(jnp.int32, (TOK, LANES), 1)
    return jnp.where(lane == 0, first, jnp.where(lane == 1, second, 0.0))


VMEM = pl.BlockSpec(memory_space=pltpu.VMEM)
ANY = pl.BlockSpec(memory_space=pl.ANY)
SMEM = pl.BlockSpec(memory_space=pltpu.SMEM)
DMA = pltpu.SemaphoreType.DMA


PIECES = ((0, 0, 896), (1, 896, 896), (1, 1792, 768), (1, 2560, 768))
GROUPS = (0, 3, 1, 2)
NSEM = 128


def ds(start, size, align):
    return pl.ds(pl.multiple_of(start, align), size)


def main_kernel(
    frames, batch, patches, w_in, wt, gout, gain1, bias1, dw,
    tubes, gwin, gdw, ggain, gbias, gwt,
    pv, pp, wv, wtv, wto, gov, goo, wrow, upr, upo, gain, bias,
    sa, ra, part, sb, rb, own, sc, rc, rya, ryc,
    pre, normed, act, slope, mslope, gmaps, small, stat, stat2,
    ev, sub, gp, left, leftr,
    ra2, rb2, own2, ownb, tra, tb, trb, acc, upt, ts, tr,
    load, send, recv,
):
    me = Place()
    loads = [
        pltpu.make_async_copy(gout, gov, load.at[0]),
        pltpu.make_async_copy(wt, wtv, load.at[1]),
        pltpu.make_async_copy(patches, pv, load.at[2]),
        pltpu.make_async_copy(w_in, wv, load.at[3]),
    ]
    for copy in loads:
        copy.start()
    mate = me.partner()
    zs = (me.zmove(1), me.zmove(3))
    ys = (me.ymove(1), me.ymove(3))
    mpk = [me.mpmove(k) for k in (1, 2, 3)]
    dest = me.sec * 4 + me.mp
    peers = []
    for k in range(1, 8):
        d = (dest + k) % 8
        peers.append((d, (lax.axis_index("dp"), d // 4, d % 4)))
    greet([mate, *zs, *ys, *[dev for _, dev in peers]])
    pending, number = [], {}

    def go(name, src, dst, dev):
        i = number.setdefault(name, len(number))
        copy = remote(src, dst, send.at[i], recv.at[i], dev)
        copy.start()
        pending.append(copy)
        return copy

    got_gout = go("gout", gout, goo, mate)
    got_wt = go("wt", wt, wto, mate)

    clip = lax.broadcasted_iota(jnp.int32, (16, 16), 0)
    other = lax.broadcasted_iota(jnp.int32, (16, 16), 1)
    zero = jnp.zeros((16, 16), jnp.int32)
    half_c, half_r, bat_c, bat_r = zero, zero, zero, zero
    for k in range(16):
        half_c = jnp.where(clip == k, frames[k], half_c)
        half_r = jnp.where(other == k, frames[k], half_r)
        bat_c = jnp.where(clip == k, batch[k], bat_c)
        bat_r = jnp.where(other == k, batch[k], bat_r)
    half_c = half_c.astype(F32) * 0.5
    half_r = half_r.astype(F32) * 0.5
    ends = jnp.sum(jnp.where(clip <= other, half_c, 0.0), axis=0, keepdims=True)
    starts = ends - half_r
    held = jnp.sum(jnp.where(bat_c == bat_r, half_c, 0.0), axis=0, keepdims=True)
    scale = (10.0 * 16) / (4.0 * held)
    place = clip.astype(F32)
    member = (place >= starts) & (place < ends)
    weight = jnp.sum(jnp.where(member, scale, 0.0), axis=1, keepdims=True)
    wrow[...] = jnp.broadcast_to(weight, (16, OW))
    gain[...] = gain1[...].reshape(1, W)
    bias[...] = bias1[...].reshape(1, W)

    r = lax.broadcasted_iota(jnp.int32, (TOK, TOK), 0)
    t = lax.broadcasted_iota(jnp.int32, (TOK, TOK), 1)
    token = (2 * ((r // 8) % 8) + r // 128) * 16 + 2 * (r % 8) + (r // 64) % 2
    order = jnp.where(token == t, 1.0, 0.0).astype(BF16)

    def pair_of(slot):
        zr, yr, cr = slot // 4, (slot // 2) % 2, slot % 2
        yh = me.yh if yr == 0 else 1 - me.yh
        core = me.core if cr == 0 else 1 - me.core
        return ((me.z + zr) % 4) * 4 + yh * 2 + core

    loads[0].wait()
    for slot in range(16):
        p = pair_of(slot)
        upr[64 * slot : 64 * slot + 64] = (gov[p].astype(F32) * wrow[pl.ds(p, 1), :]).astype(BF16)
    loads[2].wait()

    @pl.loop(0, 5)
    def _(k):
        cols = ds(k * 640, 640, LANES)
        pp[0, :, cols] = jnp.dot(order, pv[:, cols], preferred_element_type=F32).astype(BF16)

    got_gout.wait_recv()
    for k in range(4):
        for q in range(2):
            p = pair_of(4 * k + 2 - 2 * q)
            upo[k, 64 * q : 64 * q + 64] = (goo[p].astype(F32) * wrow[pl.ds(p, 1), :]).astype(BF16)
    loads[1].wait()
    got_wt.wait_recv()

    def term(k, uv):
        mine = jnp.concatenate([upr[256 * k + 128 : 256 * k + 192], upr[256 * k : 256 * k + 64]], axis=0)
        return jnp.dot(mine, wtv[uv], preferred_element_type=F32) + jnp.dot(
            upo[k], wto[uv], preferred_element_type=F32
        )

    @pl.loop(0, 4)
    def _(uv):
        res = term(2, uv).astype(BF16)
        sa[0, uv] = res[:64]
        sa[1, uv] = res[64:]

    U = (slice(0, 2), slice(2, 4))

    def send_a(q):
        return [go(f"a{q}{s}", sa.at[q, U[s]], ra.at[q, U[s]], zs[s]) for s in range(2)]

    def send_b(q, s, half):
        return go(f"b{q}{s}{half}", sb.at[s, q, U[half]], rb.at[s, q, U[half]], zs[s])

    got_a = [send_a(0), None]

    @pl.loop(0, 2)
    def _(k):
        for s, step in enumerate((1, 3)):
            res = term(step, 2 * s + k)
            part[s, 0, k] = res[:64]
            part[s, 1, k] = res[64:]
            res = term(step, 2 - 2 * s + k).astype(BF16)
            sb[s, 0, 2 - 2 * s + k] = res[:64]
            sb[s, 1, 2 - 2 * s + k] = res[64:]

    got_b = [[], []]
    got_b[0] += [send_b(0, s, 1 - s) for s in range(2)]

    def add_a(q):
        for s in range(2):
            got_a[q][s].wait_recv()
            sb[s, q, U[s]] = (part[s, q] + ra[q, U[s]].astype(F32)).astype(BF16)
            got_b[q].append(send_b(q, s, s))

    loads[3].wait()
    pre[...] = jnp.dot(pp[0], wv[...], preferred_element_type=F32)

    total = pre[:, 0:LANES]
    for b in range(1, NB):
        total = total + pre[:, b * LANES : (b + 1) * LANES]
    mean = lane_sum(total) * (1.0 / W)
    total = jnp.zeros((TOK, LANES), F32)
    for b in range(NB):
        dev = pre[:, b * LANES : (b + 1) * LANES] - mean
        total = total + dev * dev
    stat[0] = across(pick_lane(mean, lane_sum(total)), 8)
    got_stat = [go(f"stat{k}", stat.at[0], stat.at[k], mpk[k - 1]) for k in (1, 2, 3)]

    add_a(0)
    got_a[1] = send_a(1)
    got_b[1] += [send_b(1, s, 1 - s) for s in range(2)]

    @pl.loop(0, 4)
    def _(uv):
        res = term(0, uv)
        own[0, uv] = res[:64]
        own[1, uv] = res[64:]

    for copy in got_stat:
        copy.wait_recv()
    means = [stat[k][0:1] for k in range(4)]
    mean = (means[0] + means[1] + means[2] + means[3]) * 0.25
    var = stat[0][1:2] + stat[1][1:2] + stat[2][1:2] + stat[3][1:2]
    for m in means:
        var = var + W * (m - mean) * (m - mean)
    rs = down(lax.rsqrt(var * (1.0 / CH) + EPS))
    mu = down(mean)

    def cut(x):
        return [[x[128 * u + 64 * v : 128 * u + 64 * v + 64] for v in (0, 1)] for u in (0, 1)]

    @pl.loop(0, NB)
    def _(b):
        cols = lanes(b)
        norm = (pre[:, cols] - mu) * rs
        normed[:, cols] = norm
        shifted = norm * gain[:, cols] + bias[:, cols]
        sig = sigmoid(shifted)
        av = shifted * sig
        act[:, cols] = av
        slope[:, cols] = sig * (1.0 + shifted * (1.0 - sig))
        avc = cut(av)
        get = neighbours(avc)
        for u in range(2):
            for v in range(2):
                mix = jnp.zeros((64, LANES), F32)
                for a in range(3):
                    for c in range(3):
                        mix = mix + dw[a, c : c + 1, cols] * get(u + a - 1, v + c - 1)
                ms = sigmoid(mix)
                mslope[pl.ds(128 * u + 64 * v, 64), cols] = ms * (1.0 + mix * (1.0 - ms))
                ev[2 * u + v, 0:64, cols] = (avc[u][v] + mix * ms).astype(BF16)

    def spot(slot, half=None):
        return ev.at[slice(0, 4) if half is None else U[half], 64 * slot : 64 * slot + 64]

    def to_mate(slot, half=None):
        return go(f"m{slot}{half}", spot(slot, half), spot(slot + 1, half), mate)

    def over_y(name, src, relay):
        return [go(f"{name}{s}", src(s), relay.at[s], ys[s]) for s in range(2)]

    def pass_y(name, got, relay, dst):
        out = []
        for s in range(2):
            got[s].wait_recv()
            out.append(go(f"{name}p{s}", relay.at[s], dst(s), ys[s]))
        return out

    got_ya = over_y("ya", lambda s: spot(0, s), rya)
    got_mate = [to_mate(0)]

    for copy in got_b[0]:
        copy.wait_recv()
    sc[...] = (own[0] + rb[0, 0].astype(F32) + rb[1, 0].astype(F32)).astype(BF16)
    got_yc = over_y("yc", lambda s: sc.at[U[s]], ryc)
    got_flip = pass_y("ya", got_ya, rya, lambda s: spot(2, s))
    add_a(1)

    def spread(slot):
        return [
            go(f"z{slot}0", spot(slot), spot(slot + 12), zs[0]),
            go(f"z{slot}1", spot(slot), spot(slot + 4), zs[1]),
        ]

    got_z = spread(0)
    got_pp = go("pp", pp.at[0], pp.at[1], mate)

    r = lax.broadcasted_iota(jnp.int32, (512, W), 0)
    ch = lax.broadcasted_iota(jnp.int32, (512, W), 1)
    group, k = r // 32, r % 32
    base = ((group // 4) * 4 + ((group // 2) % 2) * 2) * 56 + (group % 2) * 28 + k
    base = jnp.where(k < 28, base, -10000)
    for s in range(2):
        core = me.core if s == 0 else 1 - me.core
        sub[s] = jnp.where(base + core * 56 == ch, 1.0, 0.0).astype(BF16)
    upt[...] = jnp.transpose(upr[...].astype(F32)).astype(BF16)

    got_c = pass_y("yc", got_yc, ryc, lambda s: rc.at[U[s]])
    for copy in got_flip:
        copy.wait_recv()
    got_zf = spread(2)
    got_mate.append(to_mate(2))

    for copy in got_b[1]:
        copy.wait_recv()
    for uv in range(4):
        own[1, uv] = own[1, uv] + rb[0, 1, uv].astype(F32) + rb[1, 1, uv].astype(F32)
    for copy in got_c:
        copy.wait_recv()
    for uv in range(4):
        gmaps[64 * uv : 64 * uv + 64, :] = own[1, uv] + rc[uv].astype(F32)

    @pl.loop(0, NB)
    def _(b):
        cols = lanes(b)
        norm = normed[:, cols]
        gm = gmaps[:, cols]
        gmc, avc = cut(gm * mslope[:, cols]), cut(act[:, cols])
        get, geta = neighbours(gmc), neighbours(avc)
        slo = slope[:, cols]
        dws = [[dw[a, c : c + 1, cols] for c in range(3)] for a in range(3)]
        gain_sum = jnp.zeros((64, LANES), F32)
        bias_sum = jnp.zeros((64, LANES), F32)
        for u in range(2):
            for v in range(2):
                at = slice(128 * u + 64 * v, 128 * u + 64 * v + 64)
                ga = gm[at]
                for a in range(3):
                    for c in range(3):
                        ga = ga + dws[a][c] * get(u + 1 - a, v + 1 - c)
                gs = ga * slo[at]
                bias_sum = bias_sum + gs
                gain_sum = gain_sum + gs * norm[at]
                pre[pl.ds(128 * u + 64 * v, 64), cols] = gs * gain[:, cols]
        for a in range(3):
            for c in range(3):
                tot = jnp.zeros((64, LANES), F32)
                for u in range(2):
                    for v in range(2):
                        tot = tot + gmc[u][v] * geta(u + a - 1, v + c - 1)
                k = 3 * a + c
                small[k : k + 1, cols] = jnp.sum(tot, axis=0, keepdims=True)
        small[9:10, cols] = jnp.sum(gain_sum, axis=0, keepdims=True)
        small[10:11, cols] = jnp.sum(bias_sum, axis=0, keepdims=True)

    one = jnp.zeros((TOK, LANES), F32)
    two = jnp.zeros((TOK, LANES), F32)
    for b in range(NB):
        g = pre[:, b * LANES : (b + 1) * LANES]
        one = one + g
        two = two + g * normed[:, b * LANES : (b + 1) * LANES]
    stat2[0] = across(pick_lane(lane_sum(one), lane_sum(two)), 8)
    got_stat = [go(f"back{k}", stat2.at[0], stat2.at[k], mpk[k - 1]) for k in (1, 2, 3)]

    def onward(slot, got):
        out = []
        got[0].wait_recv()
        out.append(go(f"f{slot}0", spot(slot + 12, 0), spot(slot + 8, 0), zs[0]))
        got_mate.append(to_mate(slot + 12))
        got[1].wait_recv()
        out.append(go(f"f{slot}1", spot(slot + 4, 1), spot(slot + 8, 1), zs[1]))
        got_mate.append(to_mate(slot + 4))
        return out

    def gather_end(slot, got):
        for s in range(2):
            got[s].wait_recv()
            got_mate.append(to_mate(slot + 8, s))

    got_f = onward(0, got_z)

    def products(n, first):
        rows = slice(256 * n, 256 * n + 256)

        @pl.loop(0, 4)
        def _(uv):
            res = lax.dot_general(
                ev[uv, rows], wtv[uv], (((1,), (1,)), ((), ())), preferred_element_type=F32
            )

            @pl.when(uv == 0)
            def _():
                acc[rows] = res

            @pl.when(uv > 0)
            def _():
                acc[rows] = acc[rows] + res

            more = jnp.dot(upt[:, rows], ev[uv, rows], preferred_element_type=F32)
            gwt[uv] = more if first else gwt[uv] + more

    for copy in got_mate[:2]:
        copy.wait_recv()
    products(0, True)

    for copy in got_stat:
        copy.wait_recv()
    total = stat2[0] + stat2[1] + stat2[2] + stat2[3]
    m1 = down(total[0:1] * (1.0 / CH))
    m2 = down(total[1:2] * (1.0 / CH))

    @pl.loop(0, NB)
    def _(b):
        cols = lanes(b)
        out = (pre[:, cols] - m1 - normed[:, cols] * m2) * rs
        gp[0:TOK, cols] = out.astype(BF16)
        row = lax.broadcasted_iota(jnp.int32, (16, LANES), 0)
        val = jnp.where(row < 11, small[:, cols], 0.0)
        high = val.astype(BF16)
        gp[TOK : TOK + 16, cols] = high
        gp[TOK + 64 : TOK + 80, cols] = (val - high.astype(F32)).astype(BF16)

    for at in (16, 80):
        gp[TOK + at : TOK + at + 48, :] = jnp.zeros((48, W), BF16)

    def turn(s):
        return lax.dot_general(
            sub[s], gp[...], (((1,), (1,)), ((), ())), preferred_element_type=F32
        ).astype(BF16)

    left[1] = turn(1)
    got_left = go("left", left.at[1], leftr, mate)
    left[0] = turn(0)
    got_pp.wait_recv()
    got_left.wait_recv()

    coord = (me.z, me.y)
    move = (zs, ys)
    got1, got2, got3, got4 = {}, {}, {}, {}

    def gw_at(k, start, size):
        return wv.at[ds(512 * k + start, size, 32), 0 : PIECES[k][2]]

    def sb_at(k, s, b, size):
        return wv.at[2048 + 128 * k + 64 * s + b : 2048 + 128 * k + 64 * s + b + size, 0 : PIECES[k][2]]

    def stage1(k):
        h, first, n = PIECES[k]
        grad = min(first + n, D) - first
        res = jnp.dot(left[0, :, 0:TOK], pp[0, :, first : first + grad], preferred_element_type=F32)
        res = res + jnp.dot(leftr[:, 0:TOK], pp[1, :, first : first + grad], preferred_element_type=F32)
        if grad < n:
            tail = left[0, :, TOK : TOK + LANES].astype(F32) + leftr[:, TOK : TOK + LANES].astype(F32)
            res = jnp.concatenate([res, tail], axis=1)
        res = to_link(res, grad)
        if h == 0:
            wv[512 * k : 512 * k + 512, 0:n] = res
        else:
            for a in range(4):
                for b in range(4):
                    to = 512 * k + 32 * (4 * a + b)
                    wv[to : to + 32, 0:n] = res[32 * (4 * b + a) : 32 * (4 * b + a) + 32]
        far = 128 * ((coord[h] + 2) % 4)
        got1[k] = [
            go(f"A{k}{s}", gw_at(k, far + 64 * s, 64), ra2.at[k, 64 * s : 64 * s + 64, 0:n], move[h][s])
            for s in range(2)
        ]
        got2[k] = []
        for s in range(2):
            near = 128 * ((coord[h] + 1 + 2 * s) % 4)
            rows = slice(64 - 64 * s, 128 - 64 * s)
            got2[k].append(
                go(f"B{k}{s}", gw_at(k, near + 64 - 64 * s, 64), rb2.at[k, s, rows, 0:n], move[h][s])
            )

    def stage2(k):
        h, first, n = PIECES[k]
        grad = min(first + n, D) - first
        for s in range(2):
            near = 128 * ((coord[h] + 1 + 2 * s) % 4)
            rows = slice(64 * s, 64 * s + 64)
            got1[k][s].wait_recv()
            to = sb_at(k, s, 0, 64)
            val = gw_at(k, near + 64 * s, 64)[...].astype(F32) + ra2[k, rows, 0:n].astype(F32)
            to[...] = to_link(val, grad)
            got2[k].append(go(f"C{k}{s}", to, rb2.at[k, s, rows, 0:n], move[h][s]))

    def stage3(k):
        h, first, n = PIECES[k]
        o = 1 - h
        for copy in got2[k]:
            copy.wait_recv()
        val = gw_at(k, 128 * coord[h], 128)[...].astype(F32)
        val = val + rb2[k, 0, :, 0:n].astype(F32) + rb2[k, 1, :, 0:n].astype(F32)
        own2[k, :, 0:n] = val
        ownb[k, :, 0:n] = to_link(val, min(first + n, D) - first)
        far = 32 * ((coord[o] + 2) % 4)
        got3[k] = [
            go(
                f"D{k}{s}", ownb.at[k, ds(far + 16 * s, 16, 16), 0:n],
                tra.at[k, 16 * s : 16 * s + 16, 0:n], move[o][s],
            )
            for s in range(2)
        ]
        got4[k] = []
        for s in range(2):
            near = 32 * ((coord[o] + 1 + 2 * s) % 4)
            rows = slice(16 - 16 * s, 32 - 16 * s)
            got4[k].append(
                go(
                    f"E{k}{s}", ownb.at[k, ds(near + 16 - 16 * s, 16, 16), 0:n],
                    trb.at[k, s, rows, 0:n], move[o][s],
                )
            )

    def stage4(k):
        h, first, n = PIECES[k]
        o = 1 - h
        for s in range(2):
            near = 32 * ((coord[o] + 1 + 2 * s) % 4)
            rows = slice(16 * s, 16 * s + 16)
            got3[k][s].wait_recv()
            val = own2[k, ds(near + 16 * s, 16, 16), 0:n] + tra[k, rows, 0:n].astype(F32)
            tb[k, s, :, 0:n] = to_link(val, min(first + n, D) - first)
            got4[k].append(go(f"F{k}{s}", tb.at[k, s, :, 0:n], trb.at[k, s, rows, 0:n], move[o][s]))

    def stage5(k):
        h, first, n = PIECES[k]
        for copy in got4[k]:
            copy.wait_recv()
        val = own2[k, ds(32 * coord[1 - h], 32, 32), 0:n]
        val = val + trb[k, 0, :, 0:n].astype(F32) + trb[k, 1, :, 0:n].astype(F32)
        grad = min(first + n, D) - first
        gwin[:, first : first + grad] = val[0:28, 0:grad]
        if grad < n:
            tail = jnp.transpose(jnp.concatenate([val[:, grad:], jnp.zeros((96, LANES), F32)], axis=0))
            tail = tail[0:16] + tail[64:80]
            for a in range(3):
                gdw[a] = tail[3 * a : 3 * a + 3, 0:28]
            ggain[...] = tail[9:10, 0:28]
            gbias[...] = tail[10:11, 0:28]

    for k in range(4):
        stage1(k)
    gather_end(0, got_f)
    got_ff = onward(2, got_zf)
    for k in range(4):
        stage2(k)
    for copy in got_mate[2:8]:
        copy.wait_recv()
    products(3, False)
    products(1, False)
    stage3(0)
    stage3(1)
    gather_end(2, got_ff)
    stage3(2)
    stage4(0)
    stage4(1)
    for copy in got_mate[8:]:
        copy.wait_recv()
    products(2, False)

    for k in range(8):
        piece = jnp.concatenate([acc[64 * s + 8 * k : 64 * s + 8 * k + 8] for s in range(16)], axis=0)
        ts[k] = piece.astype(BF16)
    got_t = [go(f"t{k}", ts.at[d], tr.at[k], dev) for k, (d, dev) in enumerate(peers)]
    stage3(3)
    stage4(2)
    stage5(0)
    stage5(1)
    stage4(3)
    for copy in got_t:
        copy.wait_recv()
    tot = ts[dest].astype(F32)
    for k in range(7):
        tot = tot + tr[k].astype(F32)
    for s in range(16):
        tubes[pair_of(s)] = tot[8 * s : 8 * s + 8].astype(BF16)
    stage5(2)
    stage5(3)
    for copy in pending:
        copy.wait_send()


def run_main(frames, batch, patches, w_in, wt, gout, gain, bias, dw):
    sds = jax.ShapeDtypeStruct
    vm = pltpu.VMEM
    blk, half = (4, 64, W), (2, 64, W)
    return pl.pallas_call(
        main_kernel,
        out_shape=(
            sds((16, 8, OW), BF16), sds((28, D), F32), sds((3, 3, 28), F32),
            sds((1, 28), F32), sds((1, 28), F32), sds((4, OW, W), F32),
        ),
        in_specs=[SMEM, SMEM, ANY, ANY, ANY, ANY, VMEM, VMEM, VMEM],
        out_specs=(VMEM,) * 6,
        scratch_shapes=[
            vm((TOK, D), BF16), vm((2, TOK, D), BF16), vm((D, W), BF16),
            vm((4, OW, W), BF16), vm((4, OW, W), BF16),
            vm((16, 64, OW), BF16), vm((16, 64, OW), BF16), vm((16, OW), F32),
            vm((1024, OW), BF16), vm((4, 128, OW), BF16), vm((1, W), F32), vm((1, W), F32),
            vm((2, *blk), BF16), vm((2, *blk), BF16), vm((2, 2, *half), F32),
            vm((2, 2, *blk), BF16), vm((2, 2, *blk), BF16), vm((2, *blk), F32),
            vm(blk, BF16), vm(blk, BF16), vm((2, *half), BF16), vm((2, *half), BF16),
            *[vm((TOK, W), F32)] * 6, vm((16, W), F32), vm((4, 8, TOK), F32), vm((4, 8, TOK), F32),
            vm((4, 1024, W), BF16), vm((2, 512, W), BF16), vm((TOK + LANES, W), BF16),
            vm((2, 512, TOK + LANES), BF16), vm((512, TOK + LANES), BF16),
            vm((4, 128, W), BF16), vm((4, 2, 128, W), BF16), vm((4, 128, W), F32),
            vm((4, 128, W), BF16), vm((4, 32, W), BF16), vm((4, 2, 16, W), BF16),
            vm((4, 2, 32, W), BF16), vm((1024, OW), F32), vm((OW, 1024), BF16),
            vm((8, 128, OW), BF16), vm((7, 128, OW), BF16),
            DMA((4,)), DMA((NSEM,)), DMA((NSEM,)),
        ],
        compiler_params=pltpu.CompilerParams(
            collective_id=0, has_side_effects=True, vmem_limit_bytes=63 * 1024 * 1024
        ),
        name="main",
    )(frames, batch, patches, w_in, wt, gout, gain, bias, dw)


def out_kernel(a, b, c, d, e, big, ao, bo, co, do, eo, bigo, buf, sem):
    ins = [pltpu.make_async_copy(big.at[k], buf.at[k], sem.at[0, k]) for k in range(4)]
    outs = [pltpu.make_async_copy(buf.at[k], bigo.at[k], sem.at[1, k]) for k in range(4)]
    for copy in ins:
        copy.start()
    for src, dst in ((a, ao), (b, bo), (c, co)):
        dst[...] = src[...]
    do[...] = d[...].reshape(28)
    eo[...] = e[...].reshape(28)
    for k in range(4):
        ins[k].wait()
        outs[k].start()
    for k in range(4):
        outs[k].wait()


def run_out(*arrays):
    sds = jax.ShapeDtypeStruct
    shapes = [sds(x.shape, x.dtype) for x in arrays]
    shapes[3] = shapes[4] = sds((28,), F32)
    return pl.pallas_call(
        out_kernel,
        out_shape=tuple(shapes),
        in_specs=[VMEM] * 5 + [ANY],
        out_specs=tuple([VMEM] * 5 + [ANY]),
        scratch_shapes=[pltpu.VMEM((4, OW, W), F32), DMA((2, 4))],
        name="out",
    )(*arrays)


def shards(patches, w_in, ln_gain, ln_bias, dw_kernel, w_tube, grad_out, clip_frames, clip_batch):
    wt = w_tube.transpose(0, 1, 2, 4, 3).reshape(4, OW, W)
    outs = run_main(
        clip_frames, clip_batch, patches.reshape(TOK, D), w_in, wt, grad_out, ln_gain, ln_bias, dw_kernel
    )
    tubes, gwin, gdw, ggain, gbias, gwt = run_out(*outs)
    return (
        tubes, gwin.T, ggain, gbias, gdw,
        gwt.reshape(1, 2, 2, OW, W).transpose(0, 1, 2, 4, 3),
    )


def solution(mesh):
    placed = (
        P("dp", "section", None, None, None),
        P(None, "mp"),
        P("mp"),
        P("mp"),
        P(None, None, "mp"),
        P("section", None, None, "mp", "dp"),
        P(None, None, "dp"),
        P(),
        P(),
    )
    return jax.shard_map(
        shards,
        mesh=mesh,
        in_specs=placed,
        out_specs=(
            P(None, ("section", "mp"), "dp"),
            P(None, ("mp", "dp", "section")),
            P(("mp", "dp", "section")),
            P(("mp", "dp", "section")),
            P(None, None, ("mp", "dp", "section")),
            P("section", None, None, "mp", "dp"),
        ),
        check_vma=False,
    )
```

```python
import jax
import jax.numpy as jnp
from jax import lax
from jax.experimental import pallas as pl
from jax.experimental.pallas import tpu as pltpu
from jax.sharding import PartitionSpec as P

MESH = pl.DeviceIdType.MESH
F32 = jnp.float32
BF16 = jnp.bfloat16

CH = 3584
EPS = 1e-06
W = 896
D = 3200
OW = 224
TOK = 256
DX = D + 128
HX = DX // 2
LANES = 128
NB = W // LANES


class Place:
    def __init__(self):
        dp = lax.axis_index("dp")
        self.z = dp // 4
        self.yh = (dp // 2) % 2
        self.core = dp % 2
        self.sec = lax.axis_index("section")
        self.mp = lax.axis_index("mp")
        self.y = self.yh * 2 + self.sec

    def at(self, z, yh, core):
        return (z * 4 + yh * 2 + core, self.sec, self.mp)

    def zmove(self, k):
        return self.at((self.z + k) % 4, self.yh, self.core)

    def partner(self):
        return self.at(self.z, self.yh, 1 - self.core)

    def yhflip(self):
        return self.at(self.z, 1 - self.yh, self.core)

    def ymove(self, k):
        y = (self.y + k) % 4
        return (self.z * 4 + (y // 2) * 2 + self.core, y % 2, self.mp)

    def mpmove(self, k):
        return (self.z * 4 + self.yh * 2 + self.core, self.sec, (self.mp + k) % 4)


def greet(devices):
    barrier = pltpu.get_barrier_semaphore()
    for dev in devices:
        pl.semaphore_signal(barrier, inc=1, device_id=dev, device_id_type=MESH)
    pl.semaphore_wait(barrier, len(devices))


def remote(src, dst, send, recv, dev):
    return pltpu.make_async_remote_copy(
        src_ref=src, dst_ref=dst, send_sem=send, recv_sem=recv, device_id=dev, device_id_type=MESH
    )


def lanes(b):
    return pl.ds(pl.multiple_of(b * LANES, LANES), LANES)


def sigmoid(v):
    return 1.0 / (1.0 + jnp.exp(-v))


def shift_j(plane, d):
    if d == 0:
        return plane
    row = lax.broadcasted_iota(jnp.int32, plane.shape, 0) % 8
    if d < 0:
        return jnp.where(row == 0, 0.0, pltpu.roll(plane, 1, 0))
    return jnp.where(row == 7, 0.0, pltpu.roll(plane, plane.shape[0] - 1, 0))


def shift_i(plane, d):
    if d == 0:
        return plane
    blank = jnp.zeros((8, plane.shape[1]), plane.dtype)
    if d < 0:
        return jnp.concatenate([blank, plane[:-8]], axis=0)
    return jnp.concatenate([plane[8:], blank], axis=0)


def neighbours(planes):
    moved = {}

    def get(s, t):
        us, di = s % 2, s // 2
        vs, dj = t % 2, t // 2
        if (us, vs, dj) not in moved:
            moved[us, vs, dj] = shift_j(planes[us][vs], dj)
        return shift_i(moved[us, vs, dj], di)

    return get


def across(rows, width):
    return jnp.transpose(rows)[:width]


def down(row):
    return jnp.transpose(jnp.broadcast_to(row, (LANES, row.shape[1])))


def lane_sum(x):
    return jnp.sum(x, axis=1, keepdims=True)


def two_parts(x):
    full = x + pltpu.roll(x, 64, 1)
    high = full.astype(BF16).astype(F32)
    lane = lax.broadcasted_iota(jnp.int32, x.shape, 1)
    return jnp.where(lane < 64, high, full - high).astype(BF16)


def to_link(x, grad):
    if grad == x.shape[1]:
        return x.astype(BF16)
    return jnp.concatenate([x[:, :grad].astype(BF16), two_parts(x[:, grad:])], axis=1)


def pick_lane(first, second):
    lane = lax.broadcasted_iota(jnp.int32, (TOK, LANES), 1)
    return jnp.where(lane == 0, first, jnp.where(lane == 1, second, 0.0))


VMEM = pl.BlockSpec(memory_space=pltpu.VMEM)
ANY = pl.BlockSpec(memory_space=pl.ANY)
SMEM = pl.BlockSpec(memory_space=pltpu.SMEM)
DMA = pltpu.SemaphoreType.DMA


PIECES = ((0, 0, 896), (1, 896, 896), (1, 1792, 768), (1, 2560, 768))
GROUPS = (0, 3, 1, 2)
NSEM = 128


def ds(start, size, align):
    return pl.ds(pl.multiple_of(start, align), size)


def main_kernel(
    frames, batch, patches, w_in, wt, gout, gain1, bias1, dw,
    tubes, gwin, gdw, ggain, gbias, gwt,
    pv, pp, wv, wtv, wto, gov, goo, wrow, upr, upo, gain, bias,
    sf, rf, farp, sa, ra, part, sb, rb, own, sc, rc, rya, ryc, ryf,
    pre, normed, act, slope, mslope, gmaps, small, stat, stat2,
    ev, sub, gp, left, leftr,
    ra2, rb2, own2, ownb, tra, tb, trb, acc, gacc, upt, ts, tr,
    load, send, recv,
):
    me = Place()
    loads = [
        pltpu.make_async_copy(gout, gov, load.at[0]),
        pltpu.make_async_copy(wt, wtv, load.at[1]),
        pltpu.make_async_copy(patches, pv, load.at[2]),
        pltpu.make_async_copy(w_in, wv, load.at[3]),
    ]
    for copy in loads:
        copy.start()
    mate = me.partner()
    zs = (me.zmove(1), me.zmove(3))
    ys = (me.ymove(1), me.ymove(3))
    mpk = [me.mpmove(k) for k in (1, 2, 3)]
    dest = me.sec * 4 + me.mp
    peers = []
    for k in range(1, 8):
        d = (dest + k) % 8
        peers.append((d, (lax.axis_index("dp"), d // 4, d % 4)))
    greet([mate, *zs, *ys, *[dev for _, dev in peers]])
    pending, number = [], {}

    def go(name, src, dst, dev):
        i = number.setdefault(name, len(number))
        copy = remote(src, dst, send.at[i], recv.at[i], dev)
        copy.start()
        pending.append(copy)
        return copy

    got_gout = go("gout", gout, goo, mate)
    got_wt = [go(f"wt{k}", wt.at[k], wto.at[k], mate) for k in range(4)]

    clip = lax.broadcasted_iota(jnp.int32, (16, 16), 0)
    other = lax.broadcasted_iota(jnp.int32, (16, 16), 1)
    zero = jnp.zeros((16, 16), jnp.int32)
    half_c, half_r, bat_c, bat_r = zero, zero, zero, zero
    for k in range(16):
        half_c = jnp.where(clip == k, frames[k], half_c)
        half_r = jnp.where(other == k, frames[k], half_r)
        bat_c = jnp.where(clip == k, batch[k], bat_c)
        bat_r = jnp.where(other == k, batch[k], bat_r)
    half_c = half_c.astype(F32) * 0.5
    half_r = half_r.astype(F32) * 0.5
    ends = jnp.sum(jnp.where(clip <= other, half_c, 0.0), axis=0, keepdims=True)
    starts = ends - half_r
    held = jnp.sum(jnp.where(bat_c == bat_r, half_c, 0.0), axis=0, keepdims=True)
    scale = (10.0 * 16) / (4.0 * held)
    place = clip.astype(F32)
    member = (place >= starts) & (place < ends)
    weight = jnp.sum(jnp.where(member, scale, 0.0), axis=1, keepdims=True)
    wrow[...] = jnp.broadcast_to(weight, (16, OW))
    gain[...] = gain1[...].reshape(1, W)
    bias[...] = bias1[...].reshape(1, W)

    r = lax.broadcasted_iota(jnp.int32, (TOK, TOK), 0)
    t = lax.broadcasted_iota(jnp.int32, (TOK, TOK), 1)
    token = (2 * ((r // 8) % 8) + r // 128) * 16 + 2 * (r % 8) + (r // 64) % 2
    order = jnp.where(token == t, 1.0, 0.0).astype(BF16)

    def pair_of(slot):
        zr, yr, cr = slot // 4, (slot // 2) % 2, slot % 2
        yh = me.yh if yr == 0 else 1 - me.yh
        core = me.core if cr == 0 else 1 - me.core
        return ((me.z + zr) % 4) * 4 + yh * 2 + core

    loads[0].wait()
    for slot in range(16):
        p = pair_of(slot)
        upr[64 * slot : 64 * slot + 64] = (gov[p].astype(F32) * wrow[pl.ds(p, 1), :]).astype(BF16)
    loads[2].wait()

    @pl.loop(0, 5)
    def _(k):
        cols = ds(k * 640, 640, LANES)
        pp[0, :, cols] = jnp.dot(order, pv[:, cols], preferred_element_type=F32).astype(BF16)

    got_gout.wait_recv()
    for k in range(4):
        for q in range(2):
            p = pair_of(4 * k + 2 - 2 * q)
            upo[k, 64 * q : 64 * q + 64] = (goo[p].astype(F32) * wrow[pl.ds(p, 1), :]).astype(BF16)
    loads[1].wait()

    def term(k, uv):
        mine = jnp.concatenate([upr[256 * k + 128 : 256 * k + 192], upr[256 * k : 256 * k + 64]], axis=0)
        return jnp.dot(mine, wtv[uv], preferred_element_type=F32) + jnp.dot(
            upo[k], wto[uv], preferred_element_type=F32
        )

    U = (slice(0, 2), slice(2, 4))

    def pass_y(name, got, relay, dst):
        out = []
        for s in range(2):
            got[s].wait_recv()
            out.append(go(f"{name}p{s}", relay.at[s], dst(s), ys[s]))
        return out

    got_yf = []
    for uv in range(4):
        got_wt[uv].wait_recv()
        res = term(2, uv)
        sf[uv] = res[:64].astype(BF16)
        farp[uv] = res[64:]
        if uv % 2 == 1:
            s = uv // 2
            got_yf.append(go(f"yf{s}", sf.at[U[s]], ryf.at[s], ys[s]))

    @pl.loop(0, 2)
    def _(k):
        for s, step in enumerate((1, 3)):
            res = term(step, 2 * s + k)
            sb[s, 0, 2 * s + k] = res[:64].astype(BF16)
            part[s, k] = res[64:]
            res = term(step, 2 - 2 * s + k).astype(BF16)
            sb[s, 0, 2 - 2 * s + k] = res[:64]
            sb[s, 1, 2 - 2 * s + k] = res[64:]

    got_b0 = [go(f"b0{s}", sb.at[s, 0], rb.at[s, 0], zs[s]) for s in range(2)]

    def send_b(s, half):
        return go(f"b1{s}{half}", sb.at[s, 1, U[half]], rb.at[s, 1, U[half]], zs[s])

    got_b1 = [send_b(s, 1 - s) for s in range(2)]

    loads[3].wait()
    pre[...] = jnp.dot(pp[0], wv[...], preferred_element_type=F32)

    total = pre[:, 0:LANES]
    for b in range(1, NB):
        total = total + pre[:, b * LANES : (b + 1) * LANES]
    mean = lane_sum(total) * (1.0 / W)
    total = jnp.zeros((TOK, LANES), F32)
    for b in range(NB):
        dev = pre[:, b * LANES : (b + 1) * LANES] - mean
        total = total + dev * dev
    stat[0] = across(pick_lane(mean, lane_sum(total)), 8)
    got_stat = [go(f"stat{k}", stat.at[0], stat.at[k], mpk[k - 1]) for k in (1, 2, 3)]

    got_f1 = pass_y("yf", got_yf, ryf, lambda s: rf.at[U[s]])

    @pl.loop(0, 4)
    def _(uv):
        res = term(0, uv)
        own[0, uv] = res[:64]
        own[1, uv] = res[64:]

    for copy in got_stat:
        copy.wait_recv()
    means = [stat[k][0:1] for k in range(4)]
    mean = (means[0] + means[1] + means[2] + means[3]) * 0.25
    var = stat[0][1:2] + stat[1][1:2] + stat[2][1:2] + stat[3][1:2]
    for m in means:
        var = var + W * (m - mean) * (m - mean)
    rs = down(lax.rsqrt(var * (1.0 / CH) + EPS))
    mu = down(mean)

    def cut(x):
        return [[x[128 * u + 64 * v : 128 * u + 64 * v + 64] for v in (0, 1)] for u in (0, 1)]

    @pl.loop(0, NB)
    def _(b):
        cols = lanes(b)
        norm = (pre[:, cols] - mu) * rs
        normed[:, cols] = norm
        shifted = norm * gain[:, cols] + bias[:, cols]
        sig = sigmoid(shifted)
        av = shifted * sig
        act[:, cols] = av
        slope[:, cols] = sig * (1.0 + shifted * (1.0 - sig))
        avc = cut(av)
        get = neighbours(avc)
        for u in range(2):
            for v in range(2):
                mix = jnp.zeros((64, LANES), F32)
                for a in range(3):
                    for c in range(3):
                        mix = mix + dw[a, c : c + 1, cols] * get(u + a - 1, v + c - 1)
                ms = sigmoid(mix)
                mslope[pl.ds(128 * u + 64 * v, 64), cols] = ms * (1.0 + mix * (1.0 - ms))
                ev[2 * u + v, 0:64, cols] = (avc[u][v] + mix * ms).astype(BF16)

    def spot(slot, half=None):
        return ev.at[slice(0, 4) if half is None else U[half], 64 * slot : 64 * slot + 64]

    def to_mate(slot, half=None):
        return go(f"m{slot}{half}", spot(slot, half), spot(slot + 1, half), mate)

    got_mate = [to_mate(0)]

    for copy in got_b0:
        copy.wait_recv()
    sc[...] = (own[0] + rb[0, 0].astype(F32) + rb[1, 0].astype(F32)).astype(BF16)
    got_yc = [go(f"yc{s}", sc.at[U[s]], ryc.at[s], ys[s]) for s in range(2)]
    got_a = []
    for s in range(2):
        got_f1[s].wait_recv()
        sa[U[s]] = (farp[U[s]] + rf[U[s]].astype(F32)).astype(BF16)
        got_a.append(go(f"a{s}", sa.at[U[s]], ra.at[U[s]], zs[s]))

    r = lax.broadcasted_iota(jnp.int32, (512, W), 0)
    ch = lax.broadcasted_iota(jnp.int32, (512, W), 1)
    group, k = r // 32, r % 32
    base = ((group // 4) * 4 + ((group // 2) % 2) * 2) * 56 + (group % 2) * 28 + k
    base = jnp.where(k < 28, base, -10000)
    for s in range(2):
        core = me.core if s == 0 else 1 - me.core
        sub[s] = jnp.where(base + core * 56 == ch, 1.0, 0.0).astype(BF16)
    upt[...] = jnp.transpose(upr[...].astype(F32)).astype(BF16)

    got_c = pass_y("yc", got_yc, ryc, lambda s: rc.at[U[s]])
    got_ya = [go(f"ya{s}", spot(0, s), rya.at[s], ys[s]) for s in range(2)]
    last = []
    for s in range(2):
        got_a[s].wait_recv()
        sb[s, 1, U[s]] = (part[s] + ra[U[s]].astype(F32)).astype(BF16)
        last.append(send_b(s, s))
    got_b1 += last

    def spread(slot):
        return [
            go(f"z{slot}0", spot(slot), spot(slot + 12), zs[0]),
            go(f"z{slot}1", spot(slot), spot(slot + 4), zs[1]),
        ]

    for copy in last:
        copy.wait_send()
    pending[:] = [copy for copy in pending if all(copy is not gone for gone in last)]
    got_z = spread(0)
    got_pp = go("pp", pp.at[0], pp.at[1], mate)

    for copy in got_b1:
        copy.wait_recv()
    for uv in range(4):
        own[1, uv] = own[1, uv] + rb[0, 1, uv].astype(F32) + rb[1, 1, uv].astype(F32)
    for copy in got_c:
        copy.wait_recv()
    for uv in range(4):
        gmaps[64 * uv : 64 * uv + 64, :] = own[1, uv] + rc[uv].astype(F32)

    @pl.loop(0, NB)
    def _(b):
        cols = lanes(b)
        norm = normed[:, cols]
        gm = gmaps[:, cols]
        gmc, avc = cut(gm * mslope[:, cols]), cut(act[:, cols])
        get, geta = neighbours(gmc), neighbours(avc)
        slo = slope[:, cols]
        dws = [[dw[a, c : c + 1, cols] for c in range(3)] for a in range(3)]
        gain_sum = jnp.zeros((64, LANES), F32)
        bias_sum = jnp.zeros((64, LANES), F32)
        for u in range(2):
            for v in range(2):
                at = slice(128 * u + 64 * v, 128 * u + 64 * v + 64)
                ga = gm[at]
                for a in range(3):
                    for c in range(3):
                        ga = ga + dws[a][c] * get(u + 1 - a, v + 1 - c)
                gs = ga * slo[at]
                bias_sum = bias_sum + gs
                gain_sum = gain_sum + gs * norm[at]
                pre[pl.ds(128 * u + 64 * v, 64), cols] = gs * gain[:, cols]
        for a in range(3):
            for c in range(3):
                tot = jnp.zeros((64, LANES), F32)
                for u in range(2):
                    for v in range(2):
                        tot = tot + gmc[u][v] * geta(u + a - 1, v + c - 1)
                k = 3 * a + c
                small[k : k + 1, cols] = jnp.sum(tot, axis=0, keepdims=True)
        small[9:10, cols] = jnp.sum(gain_sum, axis=0, keepdims=True)
        small[10:11, cols] = jnp.sum(bias_sum, axis=0, keepdims=True)

    one = jnp.zeros((TOK, LANES), F32)
    two = jnp.zeros((TOK, LANES), F32)
    for b in range(NB):
        g = pre[:, b * LANES : (b + 1) * LANES]
        one = one + g
        two = two + g * normed[:, b * LANES : (b + 1) * LANES]
    stat2[0] = across(pick_lane(lane_sum(one), lane_sum(two)), 8)
    got_stat = [go(f"back{k}", stat2.at[0], stat2.at[k], mpk[k - 1]) for k in (1, 2, 3)]

    def onward(slot, got):
        out = []
        got[0].wait_recv()
        out.append(go(f"f{slot}0", spot(slot + 12, 0), spot(slot + 8, 0), zs[0]))
        got_mate.append(to_mate(slot + 12))
        got[1].wait_recv()
        out.append(go(f"f{slot}1", spot(slot + 4, 1), spot(slot + 8, 1), zs[1]))
        got_mate.append(to_mate(slot + 4))
        return out

    def gather_end(slot, got):
        for s in range(2):
            got[s].wait_recv()
            got_mate.append(to_mate(slot + 8, s))

    got_flip = pass_y("ya", got_ya, rya, lambda s: spot(2, s))

    def tube_part(n):
        rows = slice(256 * n, 256 * n + 256)

        @pl.loop(0, 4)
        def _(uv):
            res = lax.dot_general(
                ev[uv, rows], wtv[uv], (((1,), (1,)), ((), ())), preferred_element_type=F32
            )

            @pl.when(uv == 0)
            def _():
                acc[rows] = res

            @pl.when(uv > 0)
            def _():
                acc[rows] = acc[rows] + res

    def gwt_part(n, first=False):
        rows = slice(256 * n, 256 * n + 256)

        @pl.loop(0, 4)
        def _(uv):
            more = jnp.dot(upt[:, rows], ev[uv, rows], preferred_element_type=F32)
            gacc[uv] = more if first else gacc[uv] + more

    for copy in got_stat:
        copy.wait_recv()
    total = stat2[0] + stat2[1] + stat2[2] + stat2[3]
    m1 = down(total[0:1] * (1.0 / CH))
    m2 = down(total[1:2] * (1.0 / CH))

    @pl.loop(0, NB)
    def _(b):
        cols = lanes(b)
        out = (pre[:, cols] - m1 - normed[:, cols] * m2) * rs
        gp[0:TOK, cols] = out.astype(BF16)
        row = lax.broadcasted_iota(jnp.int32, (16, LANES), 0)
        val = jnp.where(row < 11, small[:, cols], 0.0)
        high = val.astype(BF16)
        gp[TOK : TOK + 16, cols] = high
        gp[TOK + 64 : TOK + 80, cols] = (val - high.astype(F32)).astype(BF16)

    for at in (16, 80):
        gp[TOK + at : TOK + at + 48, :] = jnp.zeros((48, W), BF16)

    def turn(s):
        return lax.dot_general(
            sub[s], gp[...], (((1,), (1,)), ((), ())), preferred_element_type=F32
        ).astype(BF16)

    left[1] = turn(1)
    got_left = go("left", left.at[1], leftr, mate)
    left[0] = turn(0)
    got_pp.wait_recv()
    got_left.wait_recv()

    coord = (me.z, me.y)
    move = (zs, ys)
    got1, got2, got3, got4 = {}, {}, {}, {}

    def gw_at(k, start, size):
        return wv.at[ds(512 * k + start, size, 32), 0 : PIECES[k][2]]

    def sb_at(k, s, b, size):
        return wv.at[2048 + 128 * k + 64 * s + b : 2048 + 128 * k + 64 * s + b + size, 0 : PIECES[k][2]]

    def stage1(k):
        h, first, n = PIECES[k]
        grad = min(first + n, D) - first
        res = jnp.dot(left[0, :, 0:TOK], pp[0, :, first : first + grad], preferred_element_type=F32)
        res = res + jnp.dot(leftr[:, 0:TOK], pp[1, :, first : first + grad], preferred_element_type=F32)
        if grad < n:
            tail = left[0, :, TOK : TOK + LANES].astype(F32) + leftr[:, TOK : TOK + LANES].astype(F32)
            res = jnp.concatenate([res, tail], axis=1)
        res = to_link(res, grad)
        if h == 0:
            wv[512 * k : 512 * k + 512, 0:n] = res
        else:
            for a in range(4):
                for b in range(4):
                    to = 512 * k + 32 * (4 * a + b)
                    wv[to : to + 32, 0:n] = res[32 * (4 * b + a) : 32 * (4 * b + a) + 32]
        far = 128 * ((coord[h] + 2) % 4)
        got1[k] = [
            go(f"A{k}{s}", gw_at(k, far + 64 * s, 64), ra2.at[k, 64 * s : 64 * s + 64, 0:n], move[h][s])
            for s in range(2)
        ]
        got2[k] = []

    def stage1b(k):
        h, first, n = PIECES[k]
        for s in range(2):
            near = 128 * ((coord[h] + 1 + 2 * s) % 4)
            rows = slice(64 - 64 * s, 128 - 64 * s)
            got2[k].append(
                go(f"B{k}{s}", gw_at(k, near + 64 - 64 * s, 64), rb2.at[k, s, rows, 0:n], move[h][s])
            )

    def stage2(k):
        h, first, n = PIECES[k]
        grad = min(first + n, D) - first
        for s in range(2):
            near = 128 * ((coord[h] + 1 + 2 * s) % 4)
            rows = slice(64 * s, 64 * s + 64)
            got1[k][s].wait_recv()
            to = sb_at(k, s, 0, 64)
            val = gw_at(k, near + 64 * s, 64)[...].astype(F32) + ra2[k, rows, 0:n].astype(F32)
            to[...] = to_link(val, grad)
            got2[k].append(go(f"C{k}{s}", to, rb2.at[k, s, rows, 0:n], move[h][s]))

    def stage3(k):
        h, first, n = PIECES[k]
        o = 1 - h
        for copy in got2[k]:
            copy.wait_recv()
        val = gw_at(k, 128 * coord[h], 128)[...].astype(F32)
        val = val + rb2[k, 0, :, 0:n].astype(F32) + rb2[k, 1, :, 0:n].astype(F32)
        own2[k, :, 0:n] = val
        ownb[k, :, 0:n] = to_link(val, min(first + n, D) - first)
        far = 32 * ((coord[o] + 2) % 4)
        got3[k] = [
            go(
                f"D{k}{s}", ownb.at[k, ds(far + 16 * s, 16, 16), 0:n],
                tra.at[k, 16 * s : 16 * s + 16, 0:n], move[o][s],
            )
            for s in range(2)
        ]
        got4[k] = []
        for s in range(2):
            near = 32 * ((coord[o] + 1 + 2 * s) % 4)
            rows = slice(16 - 16 * s, 32 - 16 * s)
            got4[k].append(
                go(
                    f"E{k}{s}", ownb.at[k, ds(near + 16 - 16 * s, 16, 16), 0:n],
                    trb.at[k, s, rows, 0:n], move[o][s],
                )
            )

    def stage4(k):
        h, first, n = PIECES[k]
        o = 1 - h
        for s in range(2):
            near = 32 * ((coord[o] + 1 + 2 * s) % 4)
            rows = slice(16 * s, 16 * s + 16)
            got3[k][s].wait_recv()
            val = own2[k, ds(near + 16 * s, 16, 16), 0:n] + tra[k, rows, 0:n].astype(F32)
            tb[k, s, :, 0:n] = to_link(val, min(first + n, D) - first)
            got4[k].append(go(f"F{k}{s}", tb.at[k, s, :, 0:n], trb.at[k, s, rows, 0:n], move[o][s]))

    def stage5(k):
        h, first, n = PIECES[k]
        for copy in got4[k]:
            copy.wait_recv()
        val = own2[k, ds(32 * coord[1 - h], 32, 32), 0:n]
        val = val + trb[k, 0, :, 0:n].astype(F32) + trb[k, 1, :, 0:n].astype(F32)
        grad = min(first + n, D) - first
        gwin[:, first : first + grad] = val[0:28, 0:grad]
        if grad < n:
            tail = jnp.transpose(jnp.concatenate([val[:, grad:], jnp.zeros((96, LANES), F32)], axis=0))
            tail = tail[0:16] + tail[64:80]
            for a in range(3):
                gdw[a] = tail[3 * a : 3 * a + 3, 0:28]
            ggain[...] = tail[9, 0:28]
            gbias[...] = tail[10, 0:28]

    for copy in got_flip:
        copy.wait_recv()
    got_zf = spread(2)
    got_mate.append(to_mate(2))
    for k in (1, 0, 2, 3):
        stage1(k)
    for k in (1, 0, 2, 3):
        stage1b(k)
    got_f = onward(0, got_z)
    for copy in got_mate[:2]:
        copy.wait_recv()
    tube_part(0)
    gwt_part(0, True)
    for k in (1, 0, 2, 3):
        stage2(k)
    gather_end(0, got_f)
    got_ff = onward(2, got_zf)
    for copy in got_mate[2:8]:
        copy.wait_recv()
    tube_part(3)
    gwt_part(3)
    stage3(1)
    stage3(0)
    tube_part(1)
    gwt_part(1)
    gather_end(2, got_ff)
    stage3(2)
    stage4(1)
    stage4(0)
    for copy in got_mate[8:]:
        copy.wait_recv()
    tube_part(2)

    for k in range(8):
        piece = jnp.concatenate([acc[64 * s + 8 * k : 64 * s + 8 * k + 8] for s in range(16)], axis=0)
        ts[k] = piece.astype(BF16)
    got_t = [go(f"t{k}", ts.at[d], tr.at[k], dev) for k, (d, dev) in enumerate(peers)]
    stage3(3)
    stage4(2)
    gwt_part(2)
    keep = pltpu.make_async_copy(gacc, gwt, load.at[4])
    keep.start()
    stage4(3)
    stage5(1)
    stage5(0)
    for copy in got_t:
        copy.wait_recv()
    tot = ts[dest].astype(F32)
    for k in range(7):
        tot = tot + tr[k].astype(F32)
    for s in range(16):
        tubes[pair_of(s)] = tot[8 * s : 8 * s + 8].astype(BF16)
    stage5(2)
    stage5(3)
    for copy in pending:
        copy.wait_send()
    keep.wait()


def run_main(frames, batch, patches, w_in, wt, gout, gain, bias, dw):
    sds = jax.ShapeDtypeStruct
    vm = pltpu.VMEM
    blk, half = (4, 64, W), (2, 64, W)
    return pl.pallas_call(
        main_kernel,
        out_shape=(
            sds((16, 8, OW), BF16), sds((28, D), F32), sds((3, 3, 28), F32),
            sds((28,), F32), sds((28,), F32), sds((4, OW, W), F32),
        ),
        in_specs=[SMEM, SMEM, ANY, ANY, ANY, ANY, VMEM, VMEM, VMEM],
        out_specs=(VMEM, VMEM, VMEM, VMEM, VMEM, ANY),
        scratch_shapes=[
            vm((TOK, D), BF16), vm((2, TOK, D), BF16), vm((D, W), BF16),
            vm((4, OW, W), BF16), vm((4, OW, W), BF16),
            vm((16, 64, OW), BF16), vm((16, 64, OW), BF16), vm((16, OW), F32),
            vm((1024, OW), BF16), vm((4, 128, OW), BF16), vm((1, W), F32), vm((1, W), F32),
            vm(blk, BF16), vm(blk, BF16), vm(blk, F32), vm(blk, BF16), vm(blk, BF16), vm((2, *half), F32),
            vm((2, 2, *blk), BF16), vm((2, 2, *blk), BF16), vm((2, *blk), F32),
            vm(blk, BF16), vm(blk, BF16), *[vm((2, *half), BF16)] * 3,
            *[vm((TOK, W), F32)] * 6, vm((16, W), F32), vm((4, 8, TOK), F32), vm((4, 8, TOK), F32),
            vm((4, 1024, W), BF16), vm((2, 512, W), BF16), vm((TOK + LANES, W), BF16),
            vm((2, 512, TOK + LANES), BF16), vm((512, TOK + LANES), BF16),
            vm((4, 128, W), BF16), vm((4, 2, 128, W), BF16), vm((4, 128, W), F32),
            vm((4, 128, W), BF16), vm((4, 32, W), BF16), vm((4, 2, 16, W), BF16),
            vm((4, 2, 32, W), BF16), vm((1024, OW), F32), vm((4, OW, W), F32), vm((OW, 1024), BF16),
            vm((8, 128, OW), BF16), vm((7, 128, OW), BF16),
            DMA((5,)), DMA((NSEM,)), DMA((NSEM,)),
        ],
        compiler_params=pltpu.CompilerParams(
            collective_id=0, has_side_effects=True, vmem_limit_bytes=63 * 1024 * 1024
        ),
        name="main",
    )(frames, batch, patches, w_in, wt, gout, gain, bias, dw)


CUTS = 8


def out_kernel(*refs):
    n = 6
    srcs, outs, bufs, sem = refs[:n], refs[n : 2 * n], refs[2 * n : 3 * n], refs[3 * n]
    parts = [(a, b, c) for a, b, c in zip(srcs[:5], outs[:5], bufs[:5])]
    rows = OW // (CUTS // 4)
    for k in range(CUTS):
        at = (k * 4 // CUTS, slice(k % (CUTS // 4) * rows, k % (CUTS // 4) * rows + rows))
        parts.append((srcs[5].at[at], outs[5].at[at], bufs[5].at[at]))
    there = [pltpu.make_async_copy(a, c, sem.at[0, k]) for k, (a, b, c) in enumerate(parts)]
    back = [pltpu.make_async_copy(c, b, sem.at[1, k]) for k, (a, b, c) in enumerate(parts)]
    for copy in there[5:] + there[:5]:
        copy.start()
    for k in (*range(5, 5 + CUTS), *range(5)):
        there[k].wait()
        back[k].start()
    for copy in back:
        copy.wait()


def run_out(*arrays):
    return pl.pallas_call(
        out_kernel,
        out_shape=tuple(jax.ShapeDtypeStruct(x.shape, x.dtype) for x in arrays),
        in_specs=[ANY] * 6,
        out_specs=(ANY,) * 6,
        scratch_shapes=[*[pltpu.VMEM(x.shape, x.dtype) for x in arrays], DMA((2, 5 + CUTS))],
        name="out",
    )(*arrays)


def shards(patches, w_in, ln_gain, ln_bias, dw_kernel, w_tube, grad_out, clip_frames, clip_batch):
    wt = w_tube.transpose(0, 1, 2, 4, 3).reshape(4, OW, W)
    outs = run_main(
        clip_frames, clip_batch, patches.reshape(TOK, D), w_in, wt, grad_out, ln_gain, ln_bias, dw_kernel
    )
    tubes, gwin, gdw, ggain, gbias, gwt = run_out(*outs)
    return (
        tubes, gwin.T, ggain, gbias, gdw,
        gwt.reshape(1, 2, 2, OW, W).transpose(0, 1, 2, 4, 3),
    )


def solution(mesh):
    placed = (
        P("dp", "section", None, None, None),
        P(None, "mp"),
        P("mp"),
        P("mp"),
        P(None, None, "mp"),
        P("section", None, None, "mp", "dp"),
        P(None, None, "dp"),
        P(),
        P(),
    )
    return jax.shard_map(
        shards,
        mesh=mesh,
        in_specs=placed,
        out_specs=(
            P(None, ("section", "mp"), "dp"),
            P(None, ("mp", "dp", "section")),
            P(("mp", "dp", "section")),
            P(("mp", "dp", "section")),
            P(None, None, ("mp", "dp", "section")),
            P("section", None, None, "mp", "dp"),
        ),
        check_vma=False,
    )
```

```python
import jax
import jax.numpy as jnp
from jax import lax
from jax.experimental import pallas as pl
from jax.experimental.pallas import tpu as pltpu
from jax.sharding import PartitionSpec as P

MESH = pl.DeviceIdType.MESH
F32 = jnp.float32
BF16 = jnp.bfloat16

CH = 3584
EPS = 1e-06
W = 896
D = 3200
OW = 224
TOK = 256
DX = D + 128
HX = DX // 2
LANES = 128
NB = W // LANES


class Place:
    def __init__(self):
        dp = lax.axis_index("dp")
        self.z = dp // 4
        self.yh = (dp // 2) % 2
        self.core = dp % 2
        self.sec = lax.axis_index("section")
        self.mp = lax.axis_index("mp")
        self.y = self.yh * 2 + self.sec

    def at(self, z, yh, core):
        return (z * 4 + yh * 2 + core, self.sec, self.mp)

    def zmove(self, k):
        return self.at((self.z + k) % 4, self.yh, self.core)

    def partner(self):
        return self.at(self.z, self.yh, 1 - self.core)

    def yhflip(self):
        return self.at(self.z, 1 - self.yh, self.core)

    def ymove(self, k):
        y = (self.y + k) % 4
        return (self.z * 4 + (y // 2) * 2 + self.core, y % 2, self.mp)

    def mpmove(self, k):
        return (self.z * 4 + self.yh * 2 + self.core, self.sec, (self.mp + k) % 4)


def greet(devices):
    barrier = pltpu.get_barrier_semaphore()
    for dev in devices:
        pl.semaphore_signal(barrier, inc=1, device_id=dev, device_id_type=MESH)
    pl.semaphore_wait(barrier, len(devices))


def remote(src, dst, send, recv, dev):
    return pltpu.make_async_remote_copy(
        src_ref=src, dst_ref=dst, send_sem=send, recv_sem=recv, device_id=dev, device_id_type=MESH
    )


def lanes(b):
    return pl.ds(pl.multiple_of(b * LANES, LANES), LANES)


def sigmoid(v):
    return 1.0 / (1.0 + jnp.exp(-v))


def shift_j(plane, d):
    if d == 0:
        return plane
    row = lax.broadcasted_iota(jnp.int32, plane.shape, 0) % 8
    if d < 0:
        return jnp.where(row == 0, 0.0, pltpu.roll(plane, 1, 0))
    return jnp.where(row == 7, 0.0, pltpu.roll(plane, plane.shape[0] - 1, 0))


def shift_i(plane, d):
    if d == 0:
        return plane
    blank = jnp.zeros((8, plane.shape[1]), plane.dtype)
    if d < 0:
        return jnp.concatenate([blank, plane[:-8]], axis=0)
    return jnp.concatenate([plane[8:], blank], axis=0)


def neighbours(planes):
    moved = {}

    def get(s, t):
        us, di = s % 2, s // 2
        vs, dj = t % 2, t // 2
        if (us, vs, dj) not in moved:
            moved[us, vs, dj] = shift_j(planes[us][vs], dj)
        return shift_i(moved[us, vs, dj], di)

    return get


def across(rows, width):
    return jnp.transpose(rows)[:width]


def down(row):
    return jnp.transpose(jnp.broadcast_to(row, (LANES, row.shape[1])))


def lane_sum(x):
    return jnp.sum(x, axis=1, keepdims=True)


def two_parts(x):
    full = x + pltpu.roll(x, 64, 1)
    high = full.astype(BF16).astype(F32)
    lane = lax.broadcasted_iota(jnp.int32, x.shape, 1)
    return jnp.where(lane < 64, high, full - high).astype(BF16)


def to_link(x, grad):
    if grad == x.shape[1]:
        return x.astype(BF16)
    return jnp.concatenate([x[:, :grad].astype(BF16), two_parts(x[:, grad:])], axis=1)


def pick_lane(first, second):
    lane = lax.broadcasted_iota(jnp.int32, (TOK, LANES), 1)
    return jnp.where(lane == 0, first, jnp.where(lane == 1, second, 0.0))


VMEM = pl.BlockSpec(memory_space=pltpu.VMEM)
ANY = pl.BlockSpec(memory_space=pl.ANY)
SMEM = pl.BlockSpec(memory_space=pltpu.SMEM)
DMA = pltpu.SemaphoreType.DMA


PIECES = ((0, 0, 640), (1, 640, 896), (1, 1536, 896), (1, 2432, 896))
GROUPS = (0, 3, 1, 2)
NSEM = 113


def ds(start, size, align):
    return pl.ds(pl.multiple_of(start, align), size)


def main_kernel(
    frames, batch, patches, w_in, wt, gout, gain1, bias1, dw,
    tubes, gwin, gdw, ggain, gbias, gwt,
    pv, pp, wv, wtv, wto, gov, goo, wrow, upr, upo, gain, bias,
    sf, rf, farp, sa, ra, part, sb, rb, own, sc, rc, rya, ryc, ryf,
    pre, normed, act, slope, mslope, gmaps, small, stat, stat2,
    ev, sub, gp, left, leftr,
    ra2, rb2, own2, ownb, tra, tb, trb, acc, gacc, upt, ts, tr,
    tubesv, gwinv, gdwv, ggainv, gbiasv,
    load, send, recv,
):
    me = Place()
    loads = [
        pltpu.make_async_copy(gout, gov, load.at[0]),
        pltpu.make_async_copy(wt, wtv, load.at[1]),
        pltpu.make_async_copy(patches, pv, load.at[2]),
        pltpu.make_async_copy(w_in, wv, load.at[3]),
    ]
    for copy in loads:
        copy.start()
    mate = me.partner()
    zs = (me.zmove(1), me.zmove(3))
    ys = (me.ymove(1), me.ymove(3))
    mpk = [me.mpmove(k) for k in (1, 2, 3)]
    dest = me.sec * 4 + me.mp
    peers = []
    for k in range(1, 8):
        d = (dest + k) % 8
        peers.append((d, (lax.axis_index("dp"), d // 4, d % 4)))
    greet([mate, *zs, *ys, *[dev for _, dev in peers]])
    pending, number = [], {}

    def go(name, src, dst, dev):
        i = number.setdefault(name, len(number))
        copy = remote(src, dst, send.at[i], recv.at[i], dev)
        copy.start()
        pending.append(copy)
        return copy

    got_gout = go("gout", gout, goo, mate)
    got_wt = [go(f"wt{k}", wt.at[k], wto.at[k], mate) for k in range(4)]

    clip = lax.broadcasted_iota(jnp.int32, (16, 16), 0)
    other = lax.broadcasted_iota(jnp.int32, (16, 16), 1)
    zero = jnp.zeros((16, 16), jnp.int32)
    half_c, half_r, bat_c, bat_r = zero, zero, zero, zero
    for k in range(16):
        half_c = jnp.where(clip == k, frames[k], half_c)
        half_r = jnp.where(other == k, frames[k], half_r)
        bat_c = jnp.where(clip == k, batch[k], bat_c)
        bat_r = jnp.where(other == k, batch[k], bat_r)
    half_c = half_c.astype(F32) * 0.5
    half_r = half_r.astype(F32) * 0.5
    ends = jnp.sum(jnp.where(clip <= other, half_c, 0.0), axis=0, keepdims=True)
    starts = ends - half_r
    held = jnp.sum(jnp.where(bat_c == bat_r, half_c, 0.0), axis=0, keepdims=True)
    scale = (10.0 * 16) / (4.0 * held)
    place = clip.astype(F32)
    member = (place >= starts) & (place < ends)
    weight = jnp.sum(jnp.where(member, scale, 0.0), axis=1, keepdims=True)
    wrow[...] = jnp.broadcast_to(weight, (16, OW))
    gain[...] = gain1[...].reshape(1, W)
    bias[...] = bias1[...].reshape(1, W)

    r = lax.broadcasted_iota(jnp.int32, (TOK, TOK), 0)
    t = lax.broadcasted_iota(jnp.int32, (TOK, TOK), 1)
    token = (2 * ((r // 8) % 8) + r // 128) * 16 + 2 * (r % 8) + (r // 64) % 2
    order = jnp.where(token == t, 1.0, 0.0).astype(BF16)

    def pair_of(slot):
        zr, yr, cr = slot // 4, (slot // 2) % 2, slot % 2
        yh = me.yh if yr == 0 else 1 - me.yh
        core = me.core if cr == 0 else 1 - me.core
        return ((me.z + zr) % 4) * 4 + yh * 2 + core

    loads[0].wait()
    for slot in range(16):
        p = pair_of(slot)
        upr[64 * slot : 64 * slot + 64] = (gov[p].astype(F32) * wrow[pl.ds(p, 1), :]).astype(BF16)
    loads[2].wait()

    @pl.loop(0, 5)
    def _(k):
        cols = ds(k * 640, 640, LANES)
        pp[0, :, cols] = jnp.dot(order, pv[:, cols], preferred_element_type=F32).astype(BF16)

    got_gout.wait_recv()
    for k in range(4):
        for q in range(2):
            p = pair_of(4 * k + 2 - 2 * q)
            upo[k, 64 * q : 64 * q + 64] = (goo[p].astype(F32) * wrow[pl.ds(p, 1), :]).astype(BF16)
    loads[1].wait()

    def term(k, uv):
        mine = jnp.concatenate([upr[256 * k + 128 : 256 * k + 192], upr[256 * k : 256 * k + 64]], axis=0)
        return jnp.dot(mine, wtv[uv], preferred_element_type=F32) + jnp.dot(
            upo[k], wto[uv], preferred_element_type=F32
        )

    U = (slice(0, 2), slice(2, 4))

    def pass_y(name, got, relay, dst):
        out = []
        for s in range(2):
            got[s].wait_recv()
            out.append(go(f"{name}p{s}", relay.at[s], dst(s), ys[s]))
        return out

    for uv in range(4):
        got_wt[uv].wait_recv()
        for s, step in enumerate((1, 3)):
            res = term(step, uv)
            sb[s, 0, uv] = res[:64].astype(BF16)
            if uv // 2 == s:
                part[s, uv % 2] = res[64:]
            else:
                sb[s, 1, uv] = res[64:].astype(BF16)

    got_b0 = [go(f"b0{s}", sb.at[s, 0], rb.at[s, 0], zs[s]) for s in range(2)]

    def send_b(s, half):
        return go(f"b1{s}{half}", sb.at[s, 1, U[half]], rb.at[s, 1, U[half]], zs[s])

    got_b1 = [send_b(s, 1 - s) for s in range(2)]

    @pl.loop(0, 4)
    def _(uv):
        res = term(2, uv)
        sf[uv] = res[:64].astype(BF16)
        farp[uv] = res[64:]

    got_yf = [go(f"yf{s}", sf.at[U[s]], ryf.at[s], ys[s]) for s in range(2)]

    loads[3].wait()
    pre[...] = jnp.dot(pp[0], wv[...], preferred_element_type=F32)

    total = pre[:, 0:LANES]
    for b in range(1, NB):
        total = total + pre[:, b * LANES : (b + 1) * LANES]
    mean = lane_sum(total) * (1.0 / W)
    total = jnp.zeros((TOK, LANES), F32)
    for b in range(NB):
        dev = pre[:, b * LANES : (b + 1) * LANES] - mean
        total = total + dev * dev
    stat[0] = across(pick_lane(mean, lane_sum(total)), 8)
    got_stat = [go(f"stat{k}", stat.at[0], stat.at[k], mpk[k - 1]) for k in (1, 2, 3)]

    got_f1 = pass_y("yf", got_yf, ryf, lambda s: rf.at[U[s]])

    @pl.loop(0, 4)
    def _(uv):
        res = term(0, uv)
        own[0, uv] = res[:64]
        own[1, uv] = res[64:]

    for copy in got_stat:
        copy.wait_recv()
    means = [stat[k][0:1] for k in range(4)]
    mean = (means[0] + means[1] + means[2] + means[3]) * 0.25
    var = stat[0][1:2] + stat[1][1:2] + stat[2][1:2] + stat[3][1:2]
    for m in means:
        var = var + W * (m - mean) * (m - mean)
    rs = down(lax.rsqrt(var * (1.0 / CH) + EPS))
    mu = down(mean)

    def cut(x):
        return [[x[128 * u + 64 * v : 128 * u + 64 * v + 64] for v in (0, 1)] for u in (0, 1)]

    @pl.loop(0, NB)
    def _(b):
        cols = lanes(b)
        norm = (pre[:, cols] - mu) * rs
        normed[:, cols] = norm
        shifted = norm * gain[:, cols] + bias[:, cols]
        sig = sigmoid(shifted)
        av = shifted * sig
        act[:, cols] = av
        slope[:, cols] = sig * (1.0 + shifted * (1.0 - sig))
        avc = cut(av)
        get = neighbours(avc)
        for u in range(2):
            for v in range(2):
                mix = jnp.zeros((64, LANES), F32)
                for a in range(3):
                    for c in range(3):
                        mix = mix + dw[a, c : c + 1, cols] * get(u + a - 1, v + c - 1)
                ms = sigmoid(mix)
                mslope[pl.ds(128 * u + 64 * v, 64), cols] = ms * (1.0 + mix * (1.0 - ms))
                ev[2 * u + v, 0:64, cols] = (avc[u][v] + mix * ms).astype(BF16)

    def spot(slot, half=None):
        return ev.at[slice(0, 4) if half is None else U[half], 64 * slot : 64 * slot + 64]

    def to_mate(slot, half=None):
        return go(f"m{slot}{half}", spot(slot, half), spot(slot + 1, half), mate)

    got_mate = [to_mate(0)]

    for copy in got_b0:
        copy.wait_recv()
    sc[...] = (own[0] + rb[0, 0].astype(F32) + rb[1, 0].astype(F32)).astype(BF16)
    got_yc = [go(f"yc{s}", sc.at[U[s]], ryc.at[s], ys[s]) for s in range(2)]
    got_a = []
    for s in range(2):
        got_f1[s].wait_recv()
        sa[U[s]] = (farp[U[s]] + rf[U[s]].astype(F32)).astype(BF16)
        got_a.append(go(f"a{s}", sa.at[U[s]], ra.at[U[s]], zs[s]))

    r = lax.broadcasted_iota(jnp.int32, (512, W), 0)
    ch = lax.broadcasted_iota(jnp.int32, (512, W), 1)
    group, k = r // 32, r % 32
    base = ((group // 4) * 4 + ((group // 2) % 2) * 2) * 56 + (group % 2) * 28 + k
    base = jnp.where(k < 28, base, -10000)
    for s in range(2):
        core = me.core if s == 0 else 1 - me.core
        sub[s] = jnp.where(base + core * 56 == ch, 1.0, 0.0).astype(BF16)
    upt[...] = jnp.transpose(upr[...].astype(F32)).astype(BF16)

    got_c = pass_y("yc", got_yc, ryc, lambda s: rc.at[U[s]])
    got_ya = [go(f"ya{s}", spot(0, s), rya.at[s], ys[s]) for s in range(2)]
    last = []
    for s in range(2):
        got_a[s].wait_recv()
        sb[s, 1, U[s]] = (part[s] + ra[U[s]].astype(F32)).astype(BF16)
        last.append(send_b(s, s))
    got_b1 += last

    def spread(slot):
        return [
            go(f"z{slot}0", spot(slot), spot(slot + 12), zs[0]),
            go(f"z{slot}1", spot(slot), spot(slot + 4), zs[1]),
        ]

    for copy in last:
        copy.wait_send()
    pending[:] = [copy for copy in pending if all(copy is not gone for gone in last)]
    got_z = spread(0)
    got_pp = go("pp", pp.at[0], pp.at[1], mate)

    for copy in got_b1:
        copy.wait_recv()
    for uv in range(4):
        own[1, uv] = own[1, uv] + rb[0, 1, uv].astype(F32) + rb[1, 1, uv].astype(F32)
    for copy in got_c:
        copy.wait_recv()
    for uv in range(4):
        gmaps[64 * uv : 64 * uv + 64, :] = own[1, uv] + rc[uv].astype(F32)

    @pl.loop(0, NB)
    def _(b):
        cols = lanes(b)
        norm = normed[:, cols]
        gm = gmaps[:, cols]
        gmc, avc = cut(gm * mslope[:, cols]), cut(act[:, cols])
        get, geta = neighbours(gmc), neighbours(avc)
        slo = slope[:, cols]
        dws = [[dw[a, c : c + 1, cols] for c in range(3)] for a in range(3)]
        gain_sum = jnp.zeros((64, LANES), F32)
        bias_sum = jnp.zeros((64, LANES), F32)
        for u in range(2):
            for v in range(2):
                at = slice(128 * u + 64 * v, 128 * u + 64 * v + 64)
                ga = gm[at]
                for a in range(3):
                    for c in range(3):
                        ga = ga + dws[a][c] * get(u + 1 - a, v + 1 - c)
                gs = ga * slo[at]
                bias_sum = bias_sum + gs
                gain_sum = gain_sum + gs * norm[at]
                pre[pl.ds(128 * u + 64 * v, 64), cols] = gs * gain[:, cols]
        for a in range(3):
            for c in range(3):
                tot = jnp.zeros((64, LANES), F32)
                for u in range(2):
                    for v in range(2):
                        tot = tot + gmc[u][v] * geta(u + a - 1, v + c - 1)
                k = 3 * a + c
                small[k : k + 1, cols] = jnp.sum(tot, axis=0, keepdims=True)
        small[9:10, cols] = jnp.sum(gain_sum, axis=0, keepdims=True)
        small[10:11, cols] = jnp.sum(bias_sum, axis=0, keepdims=True)

    one = jnp.zeros((TOK, LANES), F32)
    two = jnp.zeros((TOK, LANES), F32)
    for b in range(NB):
        g = pre[:, b * LANES : (b + 1) * LANES]
        one = one + g
        two = two + g * normed[:, b * LANES : (b + 1) * LANES]
    stat2[0] = across(pick_lane(lane_sum(one), lane_sum(two)), 8)
    got_stat = [go(f"back{k}", stat2.at[0], stat2.at[k], mpk[k - 1]) for k in (1, 2, 3)]

    got_flip = pass_y("ya", got_ya, rya, lambda s: spot(2, s))

    def onward(slot, got):
        out = []
        got[0].wait_recv()
        out.append(go(f"f{slot}0", spot(slot + 12, 0), spot(slot + 8, 0), zs[0]))
        got_mate.append(to_mate(slot + 12))
        got[1].wait_recv()
        out.append(go(f"f{slot}1", spot(slot + 4, 1), spot(slot + 8, 1), zs[1]))
        got_mate.append(to_mate(slot + 4))
        return out

    def gather_end(slot, got):
        for s in range(2):
            got[s].wait_recv()
            got_mate.append(to_mate(slot + 8, s))

    def tube_part(n):
        rows = slice(256 * n, 256 * n + 256)

        @pl.loop(0, 4)
        def _(uv):
            res = lax.dot_general(
                ev[uv, rows], wtv[uv], (((1,), (1,)), ((), ())), preferred_element_type=F32
            )

            @pl.when(uv == 0)
            def _():
                acc[rows] = res

            @pl.when(uv > 0)
            def _():
                acc[rows] = acc[rows] + res

    def gwt_part(n, first=False):
        rows = slice(256 * n, 256 * n + 256)

        @pl.loop(0, 4)
        def _(uv):
            more = jnp.dot(upt[:, rows], ev[uv, rows], preferred_element_type=F32)
            gacc[uv] = more if first else gacc[uv] + more

    for copy in got_stat:
        copy.wait_recv()
    total = stat2[0] + stat2[1] + stat2[2] + stat2[3]
    m1 = down(total[0:1] * (1.0 / CH))
    m2 = down(total[1:2] * (1.0 / CH))

    @pl.loop(0, NB)
    def _(b):
        cols = lanes(b)
        out = (pre[:, cols] - m1 - normed[:, cols] * m2) * rs
        gp[0:TOK, cols] = out.astype(BF16)
        row = lax.broadcasted_iota(jnp.int32, (16, LANES), 0)
        val = jnp.where(row < 11, small[:, cols], 0.0)
        high = val.astype(BF16)
        gp[TOK : TOK + 16, cols] = high
        gp[TOK + 64 : TOK + 80, cols] = (val - high.astype(F32)).astype(BF16)

    for at in (16, 80):
        gp[TOK + at : TOK + at + 48, :] = jnp.zeros((48, W), BF16)

    def turn(s):
        return lax.dot_general(
            sub[s], gp[...], (((1,), (1,)), ((), ())), preferred_element_type=F32
        ).astype(BF16)

    left[1] = turn(1)
    got_left = go("left", left.at[1], leftr, mate)
    left[0] = turn(0)
    got_f = onward(0, got_z)
    for copy in got_flip:
        copy.wait_recv()
    got_zf = spread(2)
    got_mate.append(to_mate(2))
    got_pp.wait_recv()
    got_left.wait_recv()

    coord = (me.z, me.y)
    move = (zs, ys)
    got1, got2, got3, got4 = {}, {}, {}, {}

    def gw_at(k, start, size):
        return wv.at[ds(512 * k + start, size, 32), 0 : PIECES[k][2]]

    def sb_at(k, s, b, size):
        return wv.at[2048 + 128 * k + 64 * s + b : 2048 + 128 * k + 64 * s + b + size, 0 : PIECES[k][2]]

    finals = []

    def done(src, dst):
        copy = pltpu.make_async_copy(src, dst, load.at[4 + len(finals)])
        copy.start()
        finals.append(copy)

    def stage1(k):
        h, first, n = PIECES[k]
        grad = min(first + n, D) - first
        res = jnp.dot(left[0, :, 0:TOK], pp[0, :, first : first + grad], preferred_element_type=F32)
        res = res + jnp.dot(leftr[:, 0:TOK], pp[1, :, first : first + grad], preferred_element_type=F32)
        if grad < n:
            tail = left[0, :, TOK : TOK + LANES].astype(F32) + leftr[:, TOK : TOK + LANES].astype(F32)
            res = jnp.concatenate([res, tail], axis=1)
        res = to_link(res, grad)
        if h == 0:
            wv[512 * k : 512 * k + 512, 0:n] = res
        else:
            for a in range(4):
                for b in range(4):
                    to = 512 * k + 32 * (4 * a + b)
                    wv[to : to + 32, 0:n] = res[32 * (4 * b + a) : 32 * (4 * b + a) + 32]
        far = 128 * ((coord[h] + 2) % 4)
        got1[k] = [
            go(f"A{k}{s}", gw_at(k, far + 64 * s, 64), ra2.at[k, 64 * s : 64 * s + 64, 0:n], move[h][s])
            for s in range(2)
        ]
        got2[k] = []

    def stage1b(k):
        h, first, n = PIECES[k]
        for s in range(2):
            near = 128 * ((coord[h] + 1 + 2 * s) % 4)
            rows = slice(64 - 64 * s, 128 - 64 * s)
            got2[k].append(
                go(f"B{k}{s}", gw_at(k, near + 64 - 64 * s, 64), rb2.at[k, s, rows, 0:n], move[h][s])
            )

    def stage2(k):
        h, first, n = PIECES[k]
        grad = min(first + n, D) - first
        for s in range(2):
            near = 128 * ((coord[h] + 1 + 2 * s) % 4)
            rows = slice(64 * s, 64 * s + 64)
            got1[k][s].wait_recv()
            to = sb_at(k, s, 0, 64)
            val = gw_at(k, near + 64 * s, 64)[...].astype(F32) + ra2[k, rows, 0:n].astype(F32)
            to[...] = to_link(val, grad)
            got2[k].append(go(f"C{k}{s}", to, rb2.at[k, s, rows, 0:n], move[h][s]))

    def stage3(k):
        h, first, n = PIECES[k]
        o = 1 - h
        for copy in got2[k]:
            copy.wait_recv()
        val = gw_at(k, 128 * coord[h], 128)[...].astype(F32)
        val = val + rb2[k, 0, :, 0:n].astype(F32) + rb2[k, 1, :, 0:n].astype(F32)
        own2[k, :, 0:n] = val
        ownb[k, :, 0:n] = to_link(val, min(first + n, D) - first)
        far = 32 * ((coord[o] + 2) % 4)
        got3[k] = [
            go(
                f"D{k}{s}", ownb.at[k, ds(far + 16 * s, 16, 16), 0:n],
                tra.at[k, 16 * s : 16 * s + 16, 0:n], move[o][s],
            )
            for s in range(2)
        ]
        got4[k] = []
        for s in range(2):
            near = 32 * ((coord[o] + 1 + 2 * s) % 4)
            rows = slice(16 - 16 * s, 32 - 16 * s)
            got4[k].append(
                go(
                    f"E{k}{s}", ownb.at[k, ds(near + 16 - 16 * s, 16, 16), 0:n],
                    trb.at[k, s, rows, 0:n], move[o][s],
                )
            )

    def stage4(k):
        h, first, n = PIECES[k]
        o = 1 - h
        for s in range(2):
            near = 32 * ((coord[o] + 1 + 2 * s) % 4)
            rows = slice(16 * s, 16 * s + 16)
            got3[k][s].wait_recv()
            val = own2[k, ds(near + 16 * s, 16, 16), 0:n] + tra[k, rows, 0:n].astype(F32)
            tb[k, s, :, 0:n] = to_link(val, min(first + n, D) - first)
            got4[k].append(go(f"F{k}{s}", tb.at[k, s, :, 0:n], trb.at[k, s, rows, 0:n], move[o][s]))

    def stage5(k):
        h, first, n = PIECES[k]
        for copy in got4[k]:
            copy.wait_recv()
        val = own2[k, ds(32 * coord[1 - h], 32, 32), 0:n]
        val = val + trb[k, 0, :, 0:n].astype(F32) + trb[k, 1, :, 0:n].astype(F32)
        grad = min(first + n, D) - first
        gwinv[:, first : first + grad] = val[0:28, 0:grad]
        done(gwinv.at[:, first : first + grad], gwin.at[:, first : first + grad])
        if grad < n:
            tail = jnp.transpose(jnp.concatenate([val[:, grad:], jnp.zeros((96, LANES), F32)], axis=0))
            tail = tail[0:16] + tail[64:80]
            for a in range(3):
                gdwv[a] = tail[3 * a : 3 * a + 3, 0:28]
            ggainv[...] = tail[9, 0:28]
            gbiasv[...] = tail[10, 0:28]
            done(gdwv, gdw)
            done(ggainv, ggain)
            done(gbiasv, gbias)

    for k in (1, 2, 3):
        stage1(k)
    for k in (1, 2, 3):
        stage1b(k)
    stage1(0)
    stage1b(0)
    got_t = []

    def tubes_put(n):
        tube_part(n)
        at = 32 * GROUPS.index(n)
        for k in range(8):
            piece = jnp.concatenate(
                [acc[64 * s + 8 * k : 64 * s + 8 * k + 8] for s in range(4 * n, 4 * n + 4)], axis=0
            )
            ts[k, at : at + 32] = piece.astype(BF16)

    def tubes_send(name, rows):
        for k, (d, dev) in enumerate(peers):
            got_t.append(go(f"{name}{k}", ts.at[d, rows], tr.at[k, rows], dev))

    for copy in (got_mate[0], got_mate[3]):
        copy.wait_recv()
    tubes_put(0)
    gwt_part(0, True)
    stage2(1)
    stage2(2)
    stage2(3)
    got_ff = onward(2, got_zf)
    stage2(0)
    for copy in (*got_mate[1:3], *got_mate[4:6]):
        copy.wait_recv()
    tubes_put(3)
    tubes_put(1)
    tubes_send("t", slice(0, 96))
    gather_end(0, got_f)
    gwt_part(3)
    gwt_part(1)
    stage3(1)
    gather_end(2, got_ff)
    stage3(2)
    stage3(3)
    stage3(0)
    stage4(1)
    for copy in got_mate[6:]:
        copy.wait_recv()
    tubes_put(2)
    tubes_send("u", slice(96, 128))
    for k in (2, 3, 0):
        stage4(k)
    gwt_part(2)
    done(gacc, gwt)
    for k in (1, 2, 3, 0):
        stage5(k)
    for copy in got_t:
        copy.wait_recv()
    tot = ts[dest].astype(F32)
    for k in range(7):
        tot = tot + tr[k].astype(F32)
    for s in range(16):
        at = 32 * GROUPS.index(s // 4) + 8 * (s % 4)
        tubesv[pair_of(s)] = tot[at : at + 8].astype(BF16)
    done(tubesv, tubes)
    for copy in pending:
        copy.wait_send()
    for copy in finals:
        copy.wait()
    assert len(number) == NSEM, len(number)


def run_main(frames, batch, patches, w_in, wt, gout, gain, bias, dw):
    sds = jax.ShapeDtypeStruct
    vm = pltpu.VMEM
    blk, half = (4, 64, W), (2, 64, W)
    return pl.pallas_call(
        main_kernel,
        out_shape=(
            sds((16, 8, OW), BF16), sds((28, D), F32), sds((3, 3, 28), F32),
            sds((28,), F32), sds((28,), F32), sds((4, OW, W), F32),
        ),
        in_specs=[SMEM, SMEM, ANY, ANY, ANY, ANY, VMEM, VMEM, VMEM],
        out_specs=(ANY,) * 6,
        scratch_shapes=[
            vm((TOK, D), BF16), vm((2, TOK, D), BF16), vm((D, W), BF16),
            vm((4, OW, W), BF16), vm((4, OW, W), BF16),
            vm((16, 64, OW), BF16), vm((16, 64, OW), BF16), vm((16, OW), F32),
            vm((1024, OW), BF16), vm((4, 128, OW), BF16), vm((1, W), F32), vm((1, W), F32),
            vm(blk, BF16), vm(blk, BF16), vm(blk, F32), vm(blk, BF16), vm(blk, BF16), vm((2, *half), F32),
            vm((2, 2, *blk), BF16), vm((2, 2, *blk), BF16), vm((2, *blk), F32),
            vm(blk, BF16), vm(blk, BF16), *[vm((2, *half), BF16)] * 3,
            *[vm((TOK, W), F32)] * 6, vm((16, W), F32), vm((4, 8, TOK), F32), vm((4, 8, TOK), F32),
            vm((4, 1024, W), BF16), vm((2, 512, W), BF16), vm((TOK + LANES, W), BF16),
            vm((2, 512, TOK + LANES), BF16), vm((512, TOK + LANES), BF16),
            vm((4, 128, W), BF16), vm((4, 2, 128, W), BF16), vm((4, 128, W), F32),
            vm((4, 128, W), BF16), vm((4, 32, W), BF16), vm((4, 2, 16, W), BF16),
            vm((4, 2, 32, W), BF16), vm((1024, OW), F32), vm((4, OW, W), F32), vm((OW, 1024), BF16),
            vm((8, 128, OW), BF16), vm((7, 128, OW), BF16),
            vm((16, 8, OW), BF16), vm((28, D), F32), vm((3, 3, 28), F32), vm((28,), F32), vm((28,), F32),
            DMA((13,)), DMA((NSEM,)), DMA((NSEM,)),
        ],
        compiler_params=pltpu.CompilerParams(
            collective_id=0, has_side_effects=True, vmem_limit_bytes=63 * 1024 * 1024
        ),
        name="main",
    )(frames, batch, patches, w_in, wt, gout, gain, bias, dw)


CUTS = 8


def out_kernel(*refs):
    n = 6
    srcs, outs, bufs, sem = refs[:n], refs[n : 2 * n], refs[2 * n : 3 * n], refs[3 * n]
    parts = [(a, b, c) for a, b, c in zip(srcs[:5], outs[:5], bufs[:5])]
    rows = OW // (CUTS // 4)
    for k in range(CUTS):
        at = (k * 4 // CUTS, slice(k % (CUTS // 4) * rows, k % (CUTS // 4) * rows + rows))
        parts.append((srcs[5].at[at], outs[5].at[at], bufs[5].at[at]))
    there = [pltpu.make_async_copy(a, c, sem.at[0, k]) for k, (a, b, c) in enumerate(parts)]
    back = [pltpu.make_async_copy(c, b, sem.at[1, k]) for k, (a, b, c) in enumerate(parts)]
    for copy in there[5:] + there[:5]:
        copy.start()
    for k in (*range(5, 5 + CUTS), *range(5)):
        there[k].wait()
        back[k].start()
    for copy in back:
        copy.wait()


def run_out(*arrays):
    return pl.pallas_call(
        out_kernel,
        out_shape=tuple(jax.ShapeDtypeStruct(x.shape, x.dtype) for x in arrays),
        in_specs=[ANY] * 6,
        out_specs=(ANY,) * 6,
        scratch_shapes=[*[pltpu.VMEM(x.shape, x.dtype) for x in arrays], DMA((2, 5 + CUTS))],
        name="out",
    )(*arrays)


def shards(patches, w_in, ln_gain, ln_bias, dw_kernel, w_tube, grad_out, clip_frames, clip_batch):
    wt = w_tube.transpose(0, 1, 2, 4, 3).reshape(4, OW, W)
    outs = run_main(
        clip_frames, clip_batch, patches.reshape(TOK, D), w_in, wt, grad_out, ln_gain, ln_bias, dw_kernel
    )
    tubes, gwin, gdw, ggain, gbias, gwt = run_out(*outs)
    return (
        tubes, gwin.T, ggain, gbias, gdw,
        gwt.reshape(1, 2, 2, OW, W).transpose(0, 1, 2, 4, 3),
    )


def solution(mesh):
    placed = (
        P("dp", "section", None, None, None),
        P(None, "mp"),
        P("mp"),
        P("mp"),
        P(None, None, "mp"),
        P("section", None, None, "mp", "dp"),
        P(None, None, "dp"),
        P(),
        P(),
    )
    return jax.shard_map(
        shards,
        mesh=mesh,
        in_specs=placed,
        out_specs=(
            P(None, ("section", "mp"), "dp"),
            P(None, ("mp", "dp", "section")),
            P(("mp", "dp", "section")),
            P(("mp", "dp", "section")),
            P(None, None, ("mp", "dp", "section")),
            P("section", None, None, "mp", "dp"),
        ),
        check_vma=False,
    )
```

```python
import jax
import jax.numpy as jnp
from jax import lax
from jax.experimental import pallas as pl
from jax.experimental.pallas import tpu as pltpu
from jax.sharding import PartitionSpec as P

MESH = pl.DeviceIdType.MESH
F32 = jnp.float32
BF16 = jnp.bfloat16

CH = 3584
EPS = 1e-06
W = 896
D = 3200
OW = 224
TOK = 256
DX = D + 128
HX = DX // 2
LANES = 128
NB = W // LANES


class Place:
    def __init__(self):
        dp = lax.axis_index("dp")
        self.z = dp // 4
        self.yh = (dp // 2) % 2
        self.core = dp % 2
        self.sec = lax.axis_index("section")
        self.mp = lax.axis_index("mp")
        self.y = self.yh * 2 + self.sec

    def at(self, z, yh, core):
        return (z * 4 + yh * 2 + core, self.sec, self.mp)

    def zmove(self, k):
        return self.at((self.z + k) % 4, self.yh, self.core)

    def partner(self):
        return self.at(self.z, self.yh, 1 - self.core)

    def yhflip(self):
        return self.at(self.z, 1 - self.yh, self.core)

    def ymove(self, k):
        y = (self.y + k) % 4
        return (self.z * 4 + (y // 2) * 2 + self.core, y % 2, self.mp)

    def mpmove(self, k):
        return (self.z * 4 + self.yh * 2 + self.core, self.sec, (self.mp + k) % 4)


def greet(devices):
    barrier = pltpu.get_barrier_semaphore()
    for dev in devices:
        pl.semaphore_signal(barrier, inc=1, device_id=dev, device_id_type=MESH)
    pl.semaphore_wait(barrier, len(devices))


def remote(src, dst, send, recv, dev):
    return pltpu.make_async_remote_copy(
        src_ref=src, dst_ref=dst, send_sem=send, recv_sem=recv, device_id=dev, device_id_type=MESH
    )


def lanes(b):
    return pl.ds(pl.multiple_of(b * LANES, LANES), LANES)


def sigmoid(v):
    return 1.0 / (1.0 + jnp.exp(-v))


def shift_j(plane, d):
    if d == 0:
        return plane
    row = lax.broadcasted_iota(jnp.int32, plane.shape, 0) % 8
    if d < 0:
        return jnp.where(row == 0, 0.0, pltpu.roll(plane, 1, 0))
    return jnp.where(row == 7, 0.0, pltpu.roll(plane, plane.shape[0] - 1, 0))


def shift_i(plane, d):
    if d == 0:
        return plane
    blank = jnp.zeros((8, plane.shape[1]), plane.dtype)
    if d < 0:
        return jnp.concatenate([blank, plane[:-8]], axis=0)
    return jnp.concatenate([plane[8:], blank], axis=0)


def neighbours(planes):
    moved = {}

    def get(s, t):
        us, di = s % 2, s // 2
        vs, dj = t % 2, t // 2
        if (us, vs, dj) not in moved:
            moved[us, vs, dj] = shift_j(planes[us][vs], dj)
        return shift_i(moved[us, vs, dj], di)

    return get


def across(rows, width):
    return jnp.transpose(rows)[:width]


def down(row):
    return jnp.transpose(jnp.broadcast_to(row, (LANES, row.shape[1])))


def lane_sum(x):
    return jnp.sum(x, axis=1, keepdims=True)


def two_parts(x):
    full = x + pltpu.roll(x, 64, 1)
    high = full.astype(BF16).astype(F32)
    lane = lax.broadcasted_iota(jnp.int32, x.shape, 1)
    return jnp.where(lane < 64, high, full - high).astype(BF16)


def to_link(x, grad):
    if grad == x.shape[1]:
        return x.astype(BF16)
    return jnp.concatenate([x[:, :grad].astype(BF16), two_parts(x[:, grad:])], axis=1)


def pick_lane(first, second):
    lane = lax.broadcasted_iota(jnp.int32, (TOK, LANES), 1)
    return jnp.where(lane == 0, first, jnp.where(lane == 1, second, 0.0))


VMEM = pl.BlockSpec(memory_space=pltpu.VMEM)
ANY = pl.BlockSpec(memory_space=pl.ANY)
SMEM = pl.BlockSpec(memory_space=pltpu.SMEM)
DMA = pltpu.SemaphoreType.DMA


PIECES = ((0, 0, 640), (1, 640, 896), (1, 1536, 896), (1, 2432, 896))
GROUPS = (0, 3, 1, 2)
NSEM = 113
NSEND = 73


def ds(start, size, align):
    return pl.ds(pl.multiple_of(start, align), size)


def main_kernel(
    frames, batch, patches, w_in, wt, gout, gain1, bias1, dw,
    tubes, gwin, gdw, ggain, gbias, gwt,
    pv, pp, wv, wtv, wto, gov, goo, wrow, upr, upo, gain, bias,
    sf, rf, farp, sa, ra, part, sb, rb, own, sc, rc, rya, ryc, ryf,
    pre, normed, act, slope, mslope, gmaps, small, stat, stat2,
    ev, sub, gp, left, leftr,
    ra2, rb2, own2, ownb, tra, tb, trb, acc, gacc, upt, ts, tr,
    tubesv, gwinv, gdwv, ggainv, gbiasv,
    load, send, recv,
):
    me = Place()
    loads = [
        pltpu.make_async_copy(gout, gov, load.at[0]),
        pltpu.make_async_copy(wt, wtv, load.at[1]),
        pltpu.make_async_copy(patches, pv, load.at[2]),
        pltpu.make_async_copy(w_in, wv, load.at[3]),
    ]
    for copy in loads:
        copy.start()
    mate = me.partner()
    zs = (me.zmove(1), me.zmove(3))
    ys = (me.ymove(1), me.ymove(3))
    mpk = [me.mpmove(k) for k in (1, 2, 3)]
    dest = me.sec * 4 + me.mp
    peers = []
    for k in range(1, 8):
        d = (dest + k) % 8
        peers.append((d, (lax.axis_index("dp"), d // 4, d % 4)))
    greet([mate, *zs, *ys, *[dev for _, dev in peers]])
    pending, number, free, unused = [], {}, list(range(NSEND)), [NSEND]

    def go(name, src, dst, dev):
        i, k = number.setdefault(name, len(number)), free.pop(0)
        unused[0] = min(unused[0], len(free))
        copy = remote(src, dst, send.at[k], recv.at[i], dev)
        copy.start()
        pending.append((k, copy))
        return copy

    def sent(copies):
        for k, copy in list(pending):
            if any(copy is one for one in copies):
                copy.wait_send()
                free.append(k)
        pending[:] = [p for p in pending if p[0] not in free]

    got_gout = go("gout", gout, goo, mate)
    got_wt = [go(f"wt{k}", wt.at[k], wto.at[k], mate) for k in range(4)]

    clip = lax.broadcasted_iota(jnp.int32, (16, 16), 0)
    other = lax.broadcasted_iota(jnp.int32, (16, 16), 1)
    zero = jnp.zeros((16, 16), jnp.int32)
    half_c, half_r, bat_c, bat_r = zero, zero, zero, zero
    for k in range(16):
        half_c = jnp.where(clip == k, frames[k], half_c)
        half_r = jnp.where(other == k, frames[k], half_r)
        bat_c = jnp.where(clip == k, batch[k], bat_c)
        bat_r = jnp.where(other == k, batch[k], bat_r)
    half_c = half_c.astype(F32) * 0.5
    half_r = half_r.astype(F32) * 0.5
    ends = jnp.sum(jnp.where(clip <= other, half_c, 0.0), axis=0, keepdims=True)
    starts = ends - half_r
    held = jnp.sum(jnp.where(bat_c == bat_r, half_c, 0.0), axis=0, keepdims=True)
    scale = (10.0 * 16) / (4.0 * held)
    place = clip.astype(F32)
    member = (place >= starts) & (place < ends)
    weight = jnp.sum(jnp.where(member, scale, 0.0), axis=1, keepdims=True)
    wrow[...] = jnp.broadcast_to(weight, (16, OW))
    gain[...] = gain1[...].reshape(1, W)
    bias[...] = bias1[...].reshape(1, W)

    r = lax.broadcasted_iota(jnp.int32, (TOK, TOK), 0)
    t = lax.broadcasted_iota(jnp.int32, (TOK, TOK), 1)
    token = (2 * ((r // 8) % 8) + r // 128) * 16 + 2 * (r % 8) + (r // 64) % 2
    order = jnp.where(token == t, 1.0, 0.0).astype(BF16)

    def pair_of(slot):
        zr, yr, cr = slot // 4, (slot // 2) % 2, slot % 2
        yh = me.yh if yr == 0 else 1 - me.yh
        core = me.core if cr == 0 else 1 - me.core
        return ((me.z + zr) % 4) * 4 + yh * 2 + core

    loads[0].wait()
    for slot in range(16):
        p = pair_of(slot)
        upr[64 * slot : 64 * slot + 64] = (gov[p].astype(F32) * wrow[pl.ds(p, 1), :]).astype(BF16)
    loads[2].wait()

    @pl.loop(0, 5)
    def _(k):
        cols = ds(k * 640, 640, LANES)
        pp[0, :, cols] = jnp.dot(order, pv[:, cols], preferred_element_type=F32).astype(BF16)

    got_gout.wait_recv()
    for k in range(4):
        for q in range(2):
            p = pair_of(4 * k + 2 - 2 * q)
            upo[k, 64 * q : 64 * q + 64] = (goo[p].astype(F32) * wrow[pl.ds(p, 1), :]).astype(BF16)
    loads[1].wait()

    def term(k, uv):
        mine = jnp.concatenate([upr[256 * k + 128 : 256 * k + 192], upr[256 * k : 256 * k + 64]], axis=0)
        return jnp.dot(mine, wtv[uv], preferred_element_type=F32) + jnp.dot(
            upo[k], wto[uv], preferred_element_type=F32
        )

    U = (slice(0, 2), slice(2, 4))

    def pass_y(name, got, relay, dst):
        out = []
        for s in range(2):
            got[s].wait_recv()
            out.append(go(f"{name}p{s}", relay.at[s], dst(s), ys[s]))
        return out

    for uv in range(4):
        got_wt[uv].wait_recv()
        for s, step in enumerate((1, 3)):
            res = term(step, uv)
            sb[s, 0, uv] = res[:64].astype(BF16)
            if uv // 2 == s:
                part[s, uv % 2] = res[64:]
            else:
                sb[s, 1, uv] = res[64:].astype(BF16)

    got_b0 = [go(f"b0{s}", sb.at[s, 0], rb.at[s, 0], zs[s]) for s in range(2)]

    def send_b(s, half):
        return go(f"b1{s}{half}", sb.at[s, 1, U[half]], rb.at[s, 1, U[half]], zs[s])

    got_b1 = [send_b(s, 1 - s) for s in range(2)]

    @pl.loop(0, 4)
    def _(uv):
        res = term(2, uv)
        sf[uv] = res[:64].astype(BF16)
        farp[uv] = res[64:]

    got_yf = [go(f"yf{s}", sf.at[U[s]], ryf.at[s], ys[s]) for s in range(2)]

    loads[3].wait()
    pre[...] = jnp.dot(pp[0], wv[...], preferred_element_type=F32)

    total = pre[:, 0:LANES]
    for b in range(1, NB):
        total = total + pre[:, b * LANES : (b + 1) * LANES]
    mean = lane_sum(total) * (1.0 / W)
    total = jnp.zeros((TOK, LANES), F32)
    for b in range(NB):
        dev = pre[:, b * LANES : (b + 1) * LANES] - mean
        total = total + dev * dev
    stat[0] = across(pick_lane(mean, lane_sum(total)), 8)
    got_stat = [go(f"stat{k}", stat.at[0], stat.at[k], mpk[k - 1]) for k in (1, 2, 3)]

    got_f1 = pass_y("yf", got_yf, ryf, lambda s: rf.at[U[s]])

    @pl.loop(0, 4)
    def _(uv):
        res = term(0, uv)
        own[0, uv] = res[:64]
        own[1, uv] = res[64:]

    for copy in got_stat:
        copy.wait_recv()
    means = [stat[k][0:1] for k in range(4)]
    mean = (means[0] + means[1] + means[2] + means[3]) * 0.25
    var = stat[0][1:2] + stat[1][1:2] + stat[2][1:2] + stat[3][1:2]
    for m in means:
        var = var + W * (m - mean) * (m - mean)
    rs = down(lax.rsqrt(var * (1.0 / CH) + EPS))
    mu = down(mean)

    def cut(x):
        return [[x[128 * u + 64 * v : 128 * u + 64 * v + 64] for v in (0, 1)] for u in (0, 1)]

    @pl.loop(0, NB)
    def _(b):
        cols = lanes(b)
        norm = (pre[:, cols] - mu) * rs
        normed[:, cols] = norm
        shifted = norm * gain[:, cols] + bias[:, cols]
        sig = sigmoid(shifted)
        av = shifted * sig
        act[:, cols] = av
        slope[:, cols] = sig * (1.0 + shifted * (1.0 - sig))
        avc = cut(av)
        get = neighbours(avc)
        for u in range(2):
            for v in range(2):
                mix = jnp.zeros((64, LANES), F32)
                for a in range(3):
                    for c in range(3):
                        mix = mix + dw[a, c : c + 1, cols] * get(u + a - 1, v + c - 1)
                ms = sigmoid(mix)
                mslope[pl.ds(128 * u + 64 * v, 64), cols] = ms * (1.0 + mix * (1.0 - ms))
                ev[2 * u + v, 0:64, cols] = (avc[u][v] + mix * ms).astype(BF16)

    def spot(slot, half=None):
        return ev.at[slice(0, 4) if half is None else U[half], 64 * slot : 64 * slot + 64]

    def to_mate(slot, half=None):
        return go(f"m{slot}{half}", spot(slot, half), spot(slot + 1, half), mate)

    got_mate = [to_mate(0)]

    for copy in got_b0:
        copy.wait_recv()
    sc[...] = (own[0] + rb[0, 0].astype(F32) + rb[1, 0].astype(F32)).astype(BF16)
    got_yc = [go(f"yc{s}", sc.at[U[s]], ryc.at[s], ys[s]) for s in range(2)]
    got_a = []
    for s in range(2):
        got_f1[s].wait_recv()
        sa[U[s]] = (farp[U[s]] + rf[U[s]].astype(F32)).astype(BF16)
        got_a.append(go(f"a{s}", sa.at[U[s]], ra.at[U[s]], zs[s]))

    r = lax.broadcasted_iota(jnp.int32, (512, W), 0)
    ch = lax.broadcasted_iota(jnp.int32, (512, W), 1)
    group, k = r // 32, r % 32
    base = ((group // 4) * 4 + ((group // 2) % 2) * 2) * 56 + (group % 2) * 28 + k
    base = jnp.where(k < 28, base, -10000)
    for s in range(2):
        core = me.core if s == 0 else 1 - me.core
        sub[s] = jnp.where(base + core * 56 == ch, 1.0, 0.0).astype(BF16)
    upt[...] = jnp.transpose(upr[...].astype(F32)).astype(BF16)

    got_c = pass_y("yc", got_yc, ryc, lambda s: rc.at[U[s]])
    got_ya = [go(f"ya{s}", spot(0, s), rya.at[s], ys[s]) for s in range(2)]
    last = []
    for s in range(2):
        got_a[s].wait_recv()
        sb[s, 1, U[s]] = (part[s] + ra[U[s]].astype(F32)).astype(BF16)
        last.append(send_b(s, s))
    got_b1 += last

    def spread(slot):
        return [
            go(f"z{slot}0", spot(slot), spot(slot + 12), zs[0]),
            go(f"z{slot}1", spot(slot), spot(slot + 4), zs[1]),
        ]

    sent(last)
    early = [copy for _, copy in pending if all(copy is not one for one in got_ya)]
    got_z = spread(0)
    got_pp = go("pp", pp.at[0], pp.at[1], mate)

    for copy in got_b1:
        copy.wait_recv()
    for uv in range(4):
        own[1, uv] = own[1, uv] + rb[0, 1, uv].astype(F32) + rb[1, 1, uv].astype(F32)
    for copy in got_c:
        copy.wait_recv()
    for uv in range(4):
        gmaps[64 * uv : 64 * uv + 64, :] = own[1, uv] + rc[uv].astype(F32)

    sent(early)

    @pl.loop(0, NB)
    def _(b):
        cols = lanes(b)
        norm = normed[:, cols]
        gm = gmaps[:, cols]
        gmc, avc = cut(gm * mslope[:, cols]), cut(act[:, cols])
        get, geta = neighbours(gmc), neighbours(avc)
        slo = slope[:, cols]
        dws = [[dw[a, c : c + 1, cols] for c in range(3)] for a in range(3)]
        gain_sum = jnp.zeros((64, LANES), F32)
        bias_sum = jnp.zeros((64, LANES), F32)
        for u in range(2):
            for v in range(2):
                at = slice(128 * u + 64 * v, 128 * u + 64 * v + 64)
                ga = gm[at]
                for a in range(3):
                    for c in range(3):
                        ga = ga + dws[a][c] * get(u + 1 - a, v + 1 - c)
                gs = ga * slo[at]
                bias_sum = bias_sum + gs
                gain_sum = gain_sum + gs * norm[at]
                pre[pl.ds(128 * u + 64 * v, 64), cols] = gs * gain[:, cols]
        for a in range(3):
            for c in range(3):
                tot = jnp.zeros((64, LANES), F32)
                for u in range(2):
                    for v in range(2):
                        tot = tot + gmc[u][v] * geta(u + a - 1, v + c - 1)
                k = 3 * a + c
                small[k : k + 1, cols] = jnp.sum(tot, axis=0, keepdims=True)
        small[9:10, cols] = jnp.sum(gain_sum, axis=0, keepdims=True)
        small[10:11, cols] = jnp.sum(bias_sum, axis=0, keepdims=True)

    one = jnp.zeros((TOK, LANES), F32)
    two = jnp.zeros((TOK, LANES), F32)
    for b in range(NB):
        g = pre[:, b * LANES : (b + 1) * LANES]
        one = one + g
        two = two + g * normed[:, b * LANES : (b + 1) * LANES]
    stat2[0] = across(pick_lane(lane_sum(one), lane_sum(two)), 8)
    got_stat = [go(f"back{k}", stat2.at[0], stat2.at[k], mpk[k - 1]) for k in (1, 2, 3)]

    got_flip = pass_y("ya", got_ya, rya, lambda s: spot(2, s))

    def onward(slot, got):
        out = []
        got[0].wait_recv()
        out.append(go(f"f{slot}0", spot(slot + 12, 0), spot(slot + 8, 0), zs[0]))
        got_mate.append(to_mate(slot + 12))
        got[1].wait_recv()
        out.append(go(f"f{slot}1", spot(slot + 4, 1), spot(slot + 8, 1), zs[1]))
        got_mate.append(to_mate(slot + 4))
        return out

    def gather_end(slot, got):
        for s in range(2):
            got[s].wait_recv()
            got_mate.append(to_mate(slot + 8, s))

    def tube_part(n):
        rows = slice(256 * n, 256 * n + 256)

        @pl.loop(0, 4)
        def _(uv):
            res = lax.dot_general(
                ev[uv, rows], wtv[uv], (((1,), (1,)), ((), ())), preferred_element_type=F32
            )

            @pl.when(uv == 0)
            def _():
                acc[rows] = res

            @pl.when(uv > 0)
            def _():
                acc[rows] = acc[rows] + res

    def gwt_part(n, first=False):
        rows = slice(256 * n, 256 * n + 256)

        @pl.loop(0, 4)
        def _(uv):
            more = jnp.dot(upt[:, rows], ev[uv, rows], preferred_element_type=F32)
            gacc[uv] = more if first else gacc[uv] + more

    for copy in got_stat:
        copy.wait_recv()
    total = stat2[0] + stat2[1] + stat2[2] + stat2[3]
    m1 = down(total[0:1] * (1.0 / CH))
    m2 = down(total[1:2] * (1.0 / CH))

    @pl.loop(0, NB)
    def _(b):
        cols = lanes(b)
        out = (pre[:, cols] - m1 - normed[:, cols] * m2) * rs
        gp[0:TOK, cols] = out.astype(BF16)
        row = lax.broadcasted_iota(jnp.int32, (16, LANES), 0)
        val = jnp.where(row < 11, small[:, cols], 0.0)
        high = val.astype(BF16)
        gp[TOK : TOK + 16, cols] = high
        gp[TOK + 64 : TOK + 80, cols] = (val - high.astype(F32)).astype(BF16)

    for at in (16, 80):
        gp[TOK + at : TOK + at + 48, :] = jnp.zeros((48, W), BF16)

    def turn(s):
        return lax.dot_general(
            sub[s], gp[...], (((1,), (1,)), ((), ())), preferred_element_type=F32
        ).astype(BF16)

    left[1] = turn(1)
    got_left = go("left", left.at[1], leftr, mate)
    left[0] = turn(0)
    got_f = onward(0, got_z)
    for copy in got_flip:
        copy.wait_recv()
    got_zf = spread(2)
    got_mate.append(to_mate(2))
    got_pp.wait_recv()
    got_left.wait_recv()

    coord = (me.z, me.y)
    move = (zs, ys)
    got1, got2, got3, got4 = {}, {}, {}, {}

    def gw_at(k, start, size):
        return wv.at[ds(512 * k + start, size, 32), 0 : PIECES[k][2]]

    def sb_at(k, s, b, size):
        return wv.at[2048 + 128 * k + 64 * s + b : 2048 + 128 * k + 64 * s + b + size, 0 : PIECES[k][2]]

    finals = []

    def done(src, dst):
        copy = pltpu.make_async_copy(src, dst, load.at[4 + len(finals)])
        copy.start()
        finals.append(copy)

    def stage1(k):
        h, first, n = PIECES[k]
        grad = min(first + n, D) - first
        res = jnp.dot(left[0, :, 0:TOK], pp[0, :, first : first + grad], preferred_element_type=F32)
        res = res + jnp.dot(leftr[:, 0:TOK], pp[1, :, first : first + grad], preferred_element_type=F32)
        if grad < n:
            tail = left[0, :, TOK : TOK + LANES].astype(F32) + leftr[:, TOK : TOK + LANES].astype(F32)
            res = jnp.concatenate([res, tail], axis=1)
        res = to_link(res, grad)
        if h == 0:
            wv[512 * k : 512 * k + 512, 0:n] = res
        else:
            for a in range(4):
                for b in range(4):
                    to = 512 * k + 32 * (4 * a + b)
                    wv[to : to + 32, 0:n] = res[32 * (4 * b + a) : 32 * (4 * b + a) + 32]
        far = 128 * ((coord[h] + 2) % 4)
        got1[k] = [
            go(f"A{k}{s}", gw_at(k, far + 64 * s, 64), ra2.at[k, 64 * s : 64 * s + 64, 0:n], move[h][s])
            for s in range(2)
        ]
        got2[k] = []

    def stage1b(k):
        h, first, n = PIECES[k]
        for s in range(2):
            near = 128 * ((coord[h] + 1 + 2 * s) % 4)
            rows = slice(64 - 64 * s, 128 - 64 * s)
            got2[k].append(
                go(f"B{k}{s}", gw_at(k, near + 64 - 64 * s, 64), rb2.at[k, s, rows, 0:n], move[h][s])
            )

    def stage2(k):
        h, first, n = PIECES[k]
        grad = min(first + n, D) - first
        for s in range(2):
            near = 128 * ((coord[h] + 1 + 2 * s) % 4)
            rows = slice(64 * s, 64 * s + 64)
            got1[k][s].wait_recv()
            to = sb_at(k, s, 0, 64)
            val = gw_at(k, near + 64 * s, 64)[...].astype(F32) + ra2[k, rows, 0:n].astype(F32)
            to[...] = to_link(val, grad)
            got2[k].append(go(f"C{k}{s}", to, rb2.at[k, s, rows, 0:n], move[h][s]))

    def stage3(k):
        h, first, n = PIECES[k]
        o = 1 - h
        for copy in got2[k]:
            copy.wait_recv()
        val = gw_at(k, 128 * coord[h], 128)[...].astype(F32)
        val = val + rb2[k, 0, :, 0:n].astype(F32) + rb2[k, 1, :, 0:n].astype(F32)
        own2[k, :, 0:n] = val
        ownb[k, :, 0:n] = to_link(val, min(first + n, D) - first)
        far = 32 * ((coord[o] + 2) % 4)
        got3[k] = [
            go(
                f"D{k}{s}", ownb.at[k, ds(far + 16 * s, 16, 16), 0:n],
                tra.at[k, 16 * s : 16 * s + 16, 0:n], move[o][s],
            )
            for s in range(2)
        ]
        got4[k] = []
        for s in range(2):
            near = 32 * ((coord[o] + 1 + 2 * s) % 4)
            rows = slice(16 - 16 * s, 32 - 16 * s)
            got4[k].append(
                go(
                    f"E{k}{s}", ownb.at[k, ds(near + 16 - 16 * s, 16, 16), 0:n],
                    trb.at[k, s, rows, 0:n], move[o][s],
                )
            )

    def stage4(k):
        h, first, n = PIECES[k]
        o = 1 - h
        for s in range(2):
            near = 32 * ((coord[o] + 1 + 2 * s) % 4)
            rows = slice(16 * s, 16 * s + 16)
            got3[k][s].wait_recv()
            val = own2[k, ds(near + 16 * s, 16, 16), 0:n] + tra[k, rows, 0:n].astype(F32)
            tb[k, s, :, 0:n] = to_link(val, min(first + n, D) - first)
            got4[k].append(go(f"F{k}{s}", tb.at[k, s, :, 0:n], trb.at[k, s, rows, 0:n], move[o][s]))

    def stage5(k):
        h, first, n = PIECES[k]
        for copy in got4[k]:
            copy.wait_recv()
        val = own2[k, ds(32 * coord[1 - h], 32, 32), 0:n]
        val = val + trb[k, 0, :, 0:n].astype(F32) + trb[k, 1, :, 0:n].astype(F32)
        grad = min(first + n, D) - first
        gwinv[:, first : first + grad] = val[0:28, 0:grad]
        done(gwinv.at[:, first : first + grad], gwin.at[:, first : first + grad])
        if grad < n:
            tail = jnp.transpose(jnp.concatenate([val[:, grad:], jnp.zeros((96, LANES), F32)], axis=0))
            tail = tail[0:16] + tail[64:80]
            for a in range(3):
                gdwv[a] = tail[3 * a : 3 * a + 3, 0:28]
            ggainv[...] = tail[9, 0:28]
            gbiasv[...] = tail[10, 0:28]
            done(gdwv, gdw)
            done(ggainv, ggain)
            done(gbiasv, gbias)

    for k in (1, 2, 3):
        stage1(k)
    for k in (1, 2, 3):
        stage1b(k)
    stage1(0)
    stage1b(0)
    got_t = []

    def tubes_put(n):
        tube_part(n)
        at = 32 * GROUPS.index(n)
        for k in range(8):
            piece = jnp.concatenate(
                [acc[64 * s + 8 * k : 64 * s + 8 * k + 8] for s in range(4 * n, 4 * n + 4)], axis=0
            )
            ts[k, at : at + 32] = piece.astype(BF16)

    def tubes_send(name, rows):
        for k, (d, dev) in enumerate(peers):
            got_t.append(go(f"{name}{k}", ts.at[d, rows], tr.at[k, rows], dev))

    for copy in (got_mate[0], got_mate[3]):
        copy.wait_recv()
    tubes_put(0)
    gwt_part(0, True)
    stage2(1)
    stage2(2)
    stage2(3)
    got_ff = onward(2, got_zf)
    stage2(0)
    for copy in (*got_mate[1:3], *got_mate[4:6]):
        copy.wait_recv()
    early = [copy for _, copy in pending]
    tubes_put(3)
    tubes_put(1)
    tubes_send("t", slice(0, 96))
    gather_end(0, got_f)
    gwt_part(3)
    gwt_part(1)
    stage3(1)
    gather_end(2, got_ff)
    stage3(2)
    stage3(3)
    stage3(0)
    sent(early)
    stage4(1)
    for copy in got_mate[6:]:
        copy.wait_recv()
    tubes_put(2)
    tubes_send("u", slice(96, 128))
    for k in (2, 3, 0):
        stage4(k)
    gwt_part(2)
    done(gacc, gwt)
    for k in (1, 2, 3, 0):
        stage5(k)
    for copy in got_t:
        copy.wait_recv()
    tot = ts[dest].astype(F32)
    for k in range(7):
        tot = tot + tr[k].astype(F32)
    for s in range(16):
        at = 32 * GROUPS.index(s // 4) + 8 * (s % 4)
        tubesv[pair_of(s)] = tot[at : at + 8].astype(BF16)
    done(tubesv, tubes)
    for _, copy in pending:
        copy.wait_send()
    for copy in finals:
        copy.wait()
    assert len(number) == NSEM and unused[0] == 0, (len(number), unused)


def run_main(frames, batch, patches, w_in, wt, gout, gain, bias, dw):
    sds = jax.ShapeDtypeStruct
    vm = pltpu.VMEM
    blk, half = (4, 64, W), (2, 64, W)
    return pl.pallas_call(
        main_kernel,
        out_shape=(
            sds((16, 8, OW), BF16), sds((28, D), F32), sds((3, 3, 28), F32),
            sds((28,), F32), sds((28,), F32), sds((4, OW, W), F32),
        ),
        in_specs=[SMEM, SMEM, ANY, ANY, ANY, ANY, VMEM, VMEM, VMEM],
        out_specs=(ANY,) * 6,
        scratch_shapes=[
            vm((TOK, D), BF16), vm((2, TOK, D), BF16), vm((D, W), BF16),
            vm((4, OW, W), BF16), vm((4, OW, W), BF16),
            vm((16, 64, OW), BF16), vm((16, 64, OW), BF16), vm((16, OW), F32),
            vm((1024, OW), BF16), vm((4, 128, OW), BF16), vm((1, W), F32), vm((1, W), F32),
            vm(blk, BF16), vm(blk, BF16), vm(blk, F32), vm(blk, BF16), vm(blk, BF16), vm((2, *half), F32),
            vm((2, 2, *blk), BF16), vm((2, 2, *blk), BF16), vm((2, *blk), F32),
            vm(blk, BF16), vm(blk, BF16), *[vm((2, *half), BF16)] * 3,
            *[vm((TOK, W), F32)] * 6, vm((16, W), F32), vm((4, 8, TOK), F32), vm((4, 8, TOK), F32),
            vm((4, 1024, W), BF16), vm((2, 512, W), BF16), vm((TOK + LANES, W), BF16),
            vm((2, 512, TOK + LANES), BF16), vm((512, TOK + LANES), BF16),
            vm((4, 128, W), BF16), vm((4, 2, 128, W), BF16), vm((4, 128, W), F32),
            vm((4, 128, W), BF16), vm((4, 32, W), BF16), vm((4, 2, 16, W), BF16),
            vm((4, 2, 32, W), BF16), vm((1024, OW), F32), vm((4, OW, W), F32), vm((OW, 1024), BF16),
            vm((8, 128, OW), BF16), vm((7, 128, OW), BF16),
            vm((16, 8, OW), BF16), vm((28, D), F32), vm((3, 3, 28), F32), vm((28,), F32), vm((28,), F32),
            DMA((13,)), DMA((NSEND,)), DMA((NSEM,)),
        ],
        compiler_params=pltpu.CompilerParams(
            collective_id=0, has_side_effects=True, vmem_limit_bytes=63 * 1024 * 1024
        ),
        name="main",
    )(frames, batch, patches, w_in, wt, gout, gain, bias, dw)


CUTS = 8


def out_kernel(*refs):
    n = 6
    srcs, outs, bufs, sem = refs[:n], refs[n : 2 * n], refs[2 * n : 3 * n], refs[3 * n]
    parts = [(a, b, c) for a, b, c in zip(srcs[:5], outs[:5], bufs[:5])]
    rows = OW // (CUTS // 4)
    for k in range(CUTS):
        at = (k * 4 // CUTS, slice(k % (CUTS // 4) * rows, k % (CUTS // 4) * rows + rows))
        parts.append((srcs[5].at[at], outs[5].at[at], bufs[5].at[at]))
    there = [pltpu.make_async_copy(a, c, sem.at[0, k]) for k, (a, b, c) in enumerate(parts)]
    back = [pltpu.make_async_copy(c, b, sem.at[1, k]) for k, (a, b, c) in enumerate(parts)]
    for copy in there[5:] + there[:5]:
        copy.start()
    for k in (*range(5, 5 + CUTS), *range(5)):
        there[k].wait()
        back[k].start()
    for copy in back:
        copy.wait()


def run_out(*arrays):
    return pl.pallas_call(
        out_kernel,
        out_shape=tuple(jax.ShapeDtypeStruct(x.shape, x.dtype) for x in arrays),
        in_specs=[ANY] * 6,
        out_specs=(ANY,) * 6,
        scratch_shapes=[*[pltpu.VMEM(x.shape, x.dtype) for x in arrays], DMA((2, 5 + CUTS))],
        name="out",
    )(*arrays)


def shards(patches, w_in, ln_gain, ln_bias, dw_kernel, w_tube, grad_out, clip_frames, clip_batch):
    wt = w_tube.transpose(0, 1, 2, 4, 3).reshape(4, OW, W)
    outs = run_main(
        clip_frames, clip_batch, patches.reshape(TOK, D), w_in, wt, grad_out, ln_gain, ln_bias, dw_kernel
    )
    tubes, gwin, gdw, ggain, gbias, gwt = run_out(*outs)
    return (
        tubes, gwin.T, ggain, gbias, gdw,
        gwt.reshape(1, 2, 2, OW, W).transpose(0, 1, 2, 4, 3),
    )


def solution(mesh):
    placed = (
        P("dp", "section", None, None, None),
        P(None, "mp"),
        P("mp"),
        P("mp"),
        P(None, None, "mp"),
        P("section", None, None, "mp", "dp"),
        P(None, None, "dp"),
        P(),
        P(),
    )
    return jax.shard_map(
        shards,
        mesh=mesh,
        in_specs=placed,
        out_specs=(
            P(None, ("section", "mp"), "dp"),
            P(None, ("mp", "dp", "section")),
            P(("mp", "dp", "section")),
            P(("mp", "dp", "section")),
            P(None, None, ("mp", "dp", "section")),
            P("section", None, None, "mp", "dp"),
        ),
        check_vma=False,
    )
```
